32 devices in a mesh: dp: 16 (over z, y, x), mp: 2 (over core).
Axes of the slice: x: 2, y: 2, z: 4, core: 2. Of those that a mesh axis runs over, the one named last changes fastest.
Arguments:
- inputs: bfloat16 [32, 512, 768], P('dp'), may hold values from -6 to 6
- counts: int32 [32], P('dp'), may hold values from 16 to 128, as said below
- w_qkv: bfloat16 [768, 3, 768], P(None, None, 'mp'), may hold values from -0.21875 to 0.21875
- w_out: bfloat16 [768, 768], P('mp'), may hold values from -2 to 2
- w_up: bfloat16 [768, 3072], P(None, 'mp'), may hold values from -0.21875 to 0.21875
- w_down: bfloat16 [3072, 768], P('mp'), may hold values from -0.109375 to 0.109375
- gain_one: float32 [768], replicated, may hold values from 0.1 to 1.9
- shift_one: float32 [768], replicated, may hold values from -3 to 3
- gain_two: float32 [768], replicated, may hold values from 0.1 to 1.9
- shift_two: float32 [768], replicated, may hold values from -3 to 3
- cotangent: bfloat16 [32, 512, 768], P('dp'), may hold values from -6 to 6
Outputs:
- outputs: bfloat16 [32, 512, 768], P('dp')
- grad_inputs: float32 [32, 512, 768], P('dp')
- grad_w_qkv: float32 [768, 3, 768], P('dp', None, 'mp')
- grad_w_out: float32 [768, 768], P('mp', 'dp')
- grad_w_up: float32 [768, 3072], P('dp', 'mp')
- grad_w_down: float32 [3072, 768], P('mp', 'dp')
- grad_gain_one: float32 [768], P('dp')
- grad_shift_one: float32 [768], P('dp')
- grad_gain_two: float32 [768], P('dp')
- grad_shift_two: float32 [768], P('dp')
The draws below stay inside these ranges and needn't reach their ends.
Inputs may be any that keep to these rules, and one draw needn't show every extreme that they name: counts[t] is the number of live query rows of table t; some table has exactly 128.
All inputs are finite; a program needn't handle non-finite values.
Results may differ from the reference program's by a relative error of at most 0.015.
The reference program's roundings to bfloat16 on the way count: a program that leaves them out, or rounds other values in their place, can miss the bound.
Values may be sent and summed in bfloat16 or wider, within the bound.
A program may use at most 128 MiB of HBM per device.

```python
import math
import jax
import jax.numpy as jnp
from jax import lax

D = 768
H = 12
HD = 64
FF = 3072
CTX = 384
LOGQ = 7
QCAP = 128
TABLES = 32
N_MP = 2


def draw_counts(key, part):
    key_exponent, key_offset, key_full = jax.random.split(key, 3)
    exponent = jax.random.randint(key_exponent, (TABLES,), max(4, LOGQ - 2), LOGQ + 1)
    lower = jnp.left_shift(jnp.ones((TABLES,), jnp.int32), exponent - 1)
    offset = jax.random.randint(key_offset, (TABLES,), 0, 1 << 30) % (lower + 1)
    full_table = jax.random.randint(key_full, (), 0, TABLES)
    counts = jnp.where(jnp.arange(TABLES, dtype=jnp.int32) == full_table, QCAP, lower + offset)
    return counts.astype(jnp.int32)


def raised(result, own_key, source, target, parts, factor):
    def block_of(axis_at):
        return (jnp.arange(result.shape[axis_at]) // (result.shape[axis_at] // parts)).reshape((-1,) + (1,) * (result.ndim - 1 - axis_at))

    first = jax.random.permutation(own_key, parts)[block_of(target)]
    far = (block_of(target) + parts // 2) % parts
    return jnp.where((block_of(source) == first) | (block_of(source) == far), factor * result, result)


def block_scale(rng, shape, pieces, smallest, top_value):
    def one(axis_at, blocks):
        heights = jax.random.uniform(jax.random.fold_in(jax.random.fold_in(rng, 6), axis_at), (blocks,), jnp.float32, smallest / len(pieces), top_value / len(pieces))
        return jnp.repeat(jnp.exp(heights), shape[axis_at] // blocks).reshape((-1,) + (1,) * (len(shape) - axis_at - 1))

    factor_of = one(*pieces[0])
    for cut in pieces[1:]:
        factor_of = factor_of * one(*cut)
    return factor_of


def noise(own_key, shape, scale, reach, cuts=(), kind=jnp.bfloat16):
    result = jax.random.normal(own_key, shape, jnp.float32) * scale
    if len(cuts) > 0:
        result = block_scale(own_key, shape, cuts, -0.22, 0.18) * result
    return jnp.clip(result, min=-reach, max=reach).astype(kind)


def gaussian_with(stream_key, dims, deviation, most, cuts, heavy, held_as=jnp.bfloat16):
    values = deviation * jax.random.normal(stream_key, dims, jnp.float32)
    if cuts:
        values = values * block_scale(stream_key, dims, cuts, -0.22, 0.18)
    return jnp.clip(raised(values, jax.random.fold_in(stream_key, 3), *heavy), -most, most).astype(held_as)


def setup_inputs(seed: int = 0) -> dict:
    arg_keys = jax.random.split(jax.random.key(seed), 12)
    return {
        "inputs": noise(arg_keys[0], (TABLES, CTX + QCAP, D), 1.0, 6.0, ((0, 16),)),
        "counts": draw_counts(jax.random.fold_in(arg_keys[11], 71), 0),
        "w_qkv": noise(arg_keys[2], (D, 3, H * HD), D ** -0.5, 0.21875, ((2, 2),)),
        "w_out": noise(arg_keys[3], (H * HD, D), (HD // 8) ** -0.5, 2.0, ((0, 2),)),
        "w_up": noise(arg_keys[4], (D, FF), D ** -0.5, 0.21875, ((1, 2),)),
        "w_down": noise(arg_keys[5], (FF, D), FF ** -0.5, 0.109375, ((0, 2),)),
        "gain_one": jnp.clip(1.0 + 0.18 * jax.random.normal(arg_keys[6], (D,), jnp.float32), 0.1, 1.9),
        "shift_one": noise(arg_keys[7], (D,), 0.5, 3.0, (), jnp.float32),
        "gain_two": jnp.clip(1.0 + 0.18 * jax.random.normal(arg_keys[8], (D,), jnp.float32), 0.1, 1.9),
        "shift_two": noise(arg_keys[9], (D,), 0.5, 3.0, (), jnp.float32),
        "cotangent": gaussian_with(arg_keys[10], (TABLES, CTX + QCAP, D), 1.0, 6.0, ((0, 16),), (0, 2, 16, 2.0)),
    }


@jax.custom_vjp
def low(v):
    return lax.optimization_barrier(v.astype(jnp.bfloat16)).astype(jnp.float32)

@jax.custom_vjp
def low_back(v):
    return v

def low_keep(v):
    return (low(v), None)

def low_pass(kept, grad):
    return (grad,)

def back_keep(v):
    return (v, None)

def back_low(kept, grad):
    return (low(grad),)
low.defvjp(low_keep, low_pass)
low_back.defvjp(back_keep, back_low)
EPSILON = 1e-05
HIGHEST = lax.Precision.HIGHEST

def layer_norm(row_data, norm_gain, norm_shift):
    centre = lax.optimization_barrier(jnp.mean(row_data, axis=-1, keepdims=True))
    centred = row_data - centre
    variance = lax.optimization_barrier(jnp.mean(centred * centred, axis=-1, keepdims=True))
    return centred * lax.rsqrt(variance + EPSILON) * norm_gain + norm_shift

def table_layer(params, row_data):
    w_qkv, w_out, w_up, w_down, gain_one, shift_one, gain_two, shift_two = params
    seq_len = row_data.shape[0]
    score_scale = 1.0 / math.sqrt(HD)
    normed = low(layer_norm(row_data, gain_one, shift_one))
    projected = low_back(jnp.einsum('sd,dcn->scn', normed, w_qkv, precision=HIGHEST))
    query = low(projected[:, 0]).reshape(seq_len, H, HD)
    key_rows = low(projected[:CTX, 1]).reshape(CTX, H, HD)
    value_rows = low(projected[:CTX, 2]).reshape(CTX, H, HD)
    scores = low_back(jnp.einsum('shd,khd->hsk', query, key_rows, precision=HIGHEST) * score_scale)
    row_peak = lax.optimization_barrier(jnp.max(scores, axis=-1, keepdims=True))
    exp_scores = jnp.exp(scores - row_peak)
    softmax_rows = exp_scores / lax.optimization_barrier(jnp.sum(exp_scores, axis=-1, keepdims=True))
    heads_out = jnp.einsum('hsk,khd->shd', low(softmax_rows), value_rows, precision=HIGHEST)
    heads_out = low(low_back(heads_out)).reshape(seq_len, N_MP, H // N_MP * HD)
    attn_parts = jnp.einsum('smk,mkd->msd', heads_out, w_out.reshape(N_MP, H // N_MP * HD, D), precision=HIGHEST)
    resid = row_data + lax.optimization_barrier(jnp.sum(low(low_back(attn_parts)), axis=0))
    normed_two = low(layer_norm(resid, gain_two, shift_two))
    lifted = low_back(jnp.dot(normed_two, w_up, precision=HIGHEST))
    active = low(jax.nn.gelu(lifted, approximate=False))
    mlp_parts = jnp.einsum('smf,mfd->msd', active.reshape(seq_len, N_MP, FF // N_MP), w_down.reshape(N_MP, FF // N_MP, D), precision=HIGHEST)
    return resid + lax.optimization_barrier(jnp.sum(low(low_back(mlp_parts)), axis=0))

def reference(inputs, counts, w_qkv, w_out, w_up, w_down, gain_one, shift_one, gain_two, shift_two, cotangent):
    positions = jnp.arange(CTX + QCAP, dtype=jnp.int32)
    live_rows = (positions[None, :] < (CTX + counts)[:, None]).astype(jnp.float32)[:, :, None]
    params = (w_qkv.astype(jnp.float32), w_out.astype(jnp.float32), w_up.astype(jnp.float32), w_down.astype(jnp.float32), gain_one.astype(jnp.float32), shift_one.astype(jnp.float32), gain_two.astype(jnp.float32), shift_two.astype(jnp.float32))
    checked_layer = jax.checkpoint(table_layer)

    def forward(layer_params, table_data):

        def one_table(running, row_data):
            return (running, checked_layer(layer_params, row_data))
        return lax.scan(one_table, jnp.zeros((), jnp.float32), table_data)[1]
    layer_out, pullback = jax.vjp(forward, params, inputs.astype(jnp.float32))
    grads, grad_inputs = pullback(cotangent.astype(jnp.float32) * live_rows)
    outputs = (layer_out * live_rows).astype(jnp.bfloat16)
    return (outputs, grad_inputs, grads[0], grads[1], grads[2], grads[3], grads[4], grads[5], grads[6], grads[7])
```

```python
import math

import jax
import jax.numpy as jnp
from jax import lax
from jax.experimental import pallas as pl
from jax.experimental.pallas import tpu as pltpu
from jax.sharding import PartitionSpec as P

HD = 64
CTX = 384
EPS = 1e-05
BF = jnp.bfloat16
F32 = jnp.float32
MESH = pl.DeviceIdType.MESH
PAIR = 2 * HD
RB = 256


def nn(a, b):
    return lax.dot_general(a, b, (((1,), (0,)), ((), ())), preferred_element_type=F32)


def nt(a, b):
    return lax.dot_general(a, b, (((1,), (1,)), ((), ())), preferred_element_type=F32)


def unit_rows(rows):
    centre = jnp.mean(rows, axis=-1, keepdims=True)
    centred = rows - centre
    inverse = lax.rsqrt(jnp.mean(centred * centred, axis=-1, keepdims=True) + EPS)
    return centred * inverse, inverse


def norm_backward(grad, unit, inverse, gain):
    u = grad * gain
    first = jnp.mean(u, axis=-1, keepdims=True)
    second = jnp.mean(u * unit, axis=-1, keepdims=True)
    return inverse * (u - first - unit * second)


class Plan:
    def __init__(self, tables, seq, width, heads, hidden, dp):
        self.tables, self.seq, self.width, self.heads, self.hidden, self.dp = tables, seq, width, heads, hidden, dp
        self.rows = tables * seq
        self.share = width // dp
        self.fused = dp == 16 and self.share % 16 == 0
        self.step = 512 if hidden % 512 == 0 else 256
        chunks = []
        steps = hidden // self.step
        for c in range(steps):
            chunks.append(("down", c * self.step, self.step, "x"))
            chunks.append(("up", hidden + c * self.step, self.step, "y"))
        at = 2 * hidden
        for name, kind in (("out", "x"), ("q", "y"), ("k", "x"), ("v", "y")):
            chunks.append((name, at, heads, kind))
            at += heads
        chunks.append(("vec", at, 128, "x"))
        self.chunks = chunks
        self.columns = at + 128
        self.first = {name: start for name, start, _, _ in reversed(chunks)}


def layer_kernel(
    plan,
    counts_ref, x_hbm, wqkv_hbm, wout_hbm, wup_hbm, wdown_hbm, gains_hbm, cot_hbm,
    out_hbm, gin_hbm, red_hbm,
    x, wqkv, wout, wup, wdown, gains, gl,
    nrm, q, k, v, prob, ho, resid, n2, n2t, glt, act, glf, vec,
    xs, xr_a, xr_b, ms, mr,
    g, r1, r2, r3, red,
    in_sem, out_sem, xsend, xrecv, s1, q1, s2, q2, s3, q3,
):
    T, S, D, H, FF = plan.tables, plan.seq, plan.width, plan.heads, plan.hidden
    R = plan.rows
    pairs = H // PAIR
    dp = lax.axis_index("dp")
    mp = lax.axis_index("mp")
    xx, yy, zz = lax.rem(dp, 2), lax.rem(lax.div(dp, 2), 2), lax.div(dp, 4)
    partner = (dp, 1 - mp)

    def chip(z, y, x_):
        return (z * 4 + y * 2 + x_, mp)

    x_peer, y_peer = chip(zz, yy, 1 - xx), chip(zz, 1 - yy, xx)
    z_peers = [chip(lax.rem(zz + d, 4), yy, xx) for d in (1, 2, 3)]
    peers = [partner] + ([x_peer, y_peer] + z_peers if plan.fused else [])

    loads = [
        pltpu.make_async_copy(a, b, in_sem.at[i])
        for i, (a, b) in enumerate(
            ((x_hbm, x), (gains_hbm, gains), (wqkv_hbm, wqkv), (wout_hbm, wout), (cot_hbm, gl), (wup_hbm, wup), (wdown_hbm, wdown))
        )
    ]
    for c in loads:
        c.start()
    barrier = pltpu.get_barrier_semaphore()
    for n in peers:
        pl.semaphore_signal(barrier, inc=1, device_id=n, device_id_type=MESH)
    pl.semaphore_wait(barrier, len(peers))

    def remote(src, dst, ss, rs, dev):
        return pltpu.make_async_remote_copy(src, dst, ss, rs, device_id=dev, device_id_type=MESH)

    def swap(i, t, src, dst):
        rows = pl.ds(t * S, S)
        return remote(src.at[rows], dst.at[rows], xsend.at[i, t], xrecv.at[i, t], partner)

    def stages(i):
        _, c0, cw, kind = plan.chunks[i]
        cs = pl.ds(c0, cw)
        isx = kind == "x"
        other, mine = (1 - yy, yy) if isx else (1 - xx, xx)
        c1 = remote(
            g.at[:, :, 1 - xx, :, cs] if isx else g.at[:, 1 - yy, :, :, cs],
            r1.at[:, :, :, cs], s1.at[i], q1.at[i], x_peer if isx else y_peer,
        )
        c2 = remote(r1.at[:, other, :, cs], r2.at[:, :, cs], s2.at[i], q2.at[i], y_peer if isx else x_peer)
        c3 = [
            remote(r2.at[lax.rem(zz + d, 4), :, cs], r3.at[d - 1, :, cs], s3.at[i, d - 1], q3.at[i, d - 1], z_peers[d - 1])
            for d in (1, 2, 3)
        ]

        def add_one():
            c1.wait_recv()

            def part(p):
                for z in range(4):
                    own = g[z, p, xx, :, cs] if isx else g[z, yy, p, :, cs]
                    r1[z, p, :, cs] = (own.astype(F32) + r1[z, p, :, cs].astype(F32)).astype(BF)

            part(other)
            c2.start()
            part(mine)

        def add_two():
            c2.wait_recv()
            for d in (2, 3, 1, 0):
                z = lax.rem(zz + d, 4)
                r2[z, :, cs] = (r1[z, mine, :, cs].astype(F32) + r2[z, :, cs].astype(F32)).astype(BF)
                if d:
                    c3[d - 1].start()

        def add_three():
            for c in c3:
                c.wait_recv()
            total = r2[zz, :, cs].astype(F32)
            for d in range(3):
                total = total + r3[d, :, cs].astype(F32)
            red[:, cs] = total

        def drain():
            for c in (c1, c2, *c3):
                c.wait_send()

        return c1.start, add_one, add_two, add_three, drain

    ready = set()
    events = []
    if plan.fused:
        prog = [stages(i) for i in range(len(plan.chunks))]
        count = len(prog)
        window, lag = 2, 1
        for i in range(min(window, count)):
            events.append((i, prog[i][0]))
        for t in range(count + 2 * lag):
            if t < count:
                events.append((t, prog[t][1]))
                if t + window < count:
                    events.append((t + window, prog[t + window][0]))
            if 0 <= t - lag < count:
                events.append((t - lag, prog[t - lag][2]))
            if 0 <= t - 2 * lag < count:
                events.append((t - 2 * lag, prog[t - 2 * lag][3]))

    def service(n):
        while n > 0 and events and events[0][0] in ready:
            events.pop(0)[1]()
            n -= 1

    def made(name, i=0):
        for j, c in enumerate(plan.chunks):
            if c[0] == name:
                if i == 0:
                    ready.add(j)
                    return
                i -= 1

    def put(c0, cw, rows768):
        cs = pl.ds(c0, cw)
        if plan.fused:
            g[:, :, :, :, cs] = rows768.astype(BF).reshape(4, 2, 2, plan.share, cw)
        else:
            g[:, cs] = rows768.astype(BF)

    def blocks(n, body):
        def step(i, carry):
            body(i)
            return carry

        lax.fori_loop(0, n, step, 0)

    def rows_of(b):
        return pl.ds(pl.multiple_of(b * RB, RB), RB)

    loads[0].wait()
    loads[1].wait()
    g1, b1, g2, b2 = (gains[i : i + 1, :] for i in range(4))

    def first_norm(b):
        rs = rows_of(b)
        unit, _ = unit_rows(x[rs, :].astype(F32))
        nrm[rs, :] = (unit * g1 + b1).astype(BF)

    blocks(R // RB, first_norm)
    loads[2].wait()

    def project(t):
        all_rows = pl.ds(pl.multiple_of(t * S, S), S)
        context = pl.ds(pl.multiple_of(t * S, S), CTX)
        q[all_rows, :] = nn(nrm[all_rows, :], wqkv[:, 0:H]).astype(BF)
        k[context, :] = nn(nrm[context, :], wqkv[:, H : 2 * H]).astype(BF)
        v[context, :] = nn(nrm[context, :], wqkv[:, 2 * H : 3 * H]).astype(BF)

    blocks(T, project)

    scale = 1.0 / math.sqrt(HD)
    low_lane = lax.broadcasted_iota(jnp.int32, (CTX, PAIR), 1) < HD
    low_row = lax.broadcasted_iota(jnp.int32, (PAIR, CTX), 0) < HD

    def stacked(a):
        zero = jnp.zeros_like(a)
        return jnp.concatenate([jnp.where(low_lane, a, zero), jnp.where(low_lane, zero, a)], axis=0)

    def beside(a):
        at = a.T
        zero = jnp.zeros_like(at)
        return jnp.concatenate([jnp.where(low_row, at, zero), jnp.where(low_row, zero, at)], axis=1)

    def merged(a):
        return jnp.where(low_lane, a[:CTX], a[CTX:])

    def attend(t, h):
        rows = pl.ds(pl.multiple_of(t * S, S), S)
        context = pl.ds(pl.multiple_of(t * S, S), CTX)
        cols = pl.ds(pl.multiple_of(h * PAIR, PAIR), PAIR)
        slot = t * pairs + h
        scores = nt(stacked(k[context, cols]), q[rows, cols])
        halves = []
        for i in range(2):
            s = scores[i * CTX : (i + 1) * CTX]
            e = jnp.exp((s - jnp.max(s, axis=0, keepdims=True)) * scale)
            p = e * (1.0 / jnp.sum(e, axis=0, keepdims=True))
            prob[slot, i * CTX : (i + 1) * CTX, :] = p
            halves.append(p.astype(BF))
        out_t = nn(beside(v[context, cols]), jnp.concatenate(halves, axis=0))
        ho[rows, cols] = out_t.T.astype(BF)

    loads[3].wait()
    for t in range(T):
        blocks(pairs, lambda h, t=t: attend(t, h))
        rows = pl.ds(t * S, S)
        xs[rows, :] = nn(ho[rows, :], wout[...]).astype(BF)
        swap(0, t, xs, xr_a).start()

    loads[4].wait()

    def mask(b):
        rs = rows_of(b)
        pos = lax.broadcasted_iota(jnp.int32, (RB, 1), 0) + lax.rem(b * RB, S)
        live = pos < CTX + counts_ref[lax.div(b * RB, S)]
        kept = jnp.where(live, gl[rs, :].astype(F32), 0.0).astype(BF)
        gl[rs, :] = kept
        glt[:, rs] = kept.T

    blocks(R // RB, mask)

    def second_norm(b):
        rs = rows_of(b)
        r = x[rs, :].astype(F32) + (xs[rs, :].astype(F32) + xr_a[rs, :].astype(F32))
        resid[rs, :] = r
        unit, _ = unit_rows(r)
        low = (unit * g2 + b2).astype(BF)
        n2[rs, :] = low
        n2t[:, rs] = low.T

    per = S // RB
    for t in range(T):
        swap(0, t, xs, xr_a).wait_recv()
        blocks(per, lambda i, t=t: second_norm(t * per + i))
    loads[5].wait()
    loads[6].wait()

    def feed(c0, cw):
        cs = pl.ds(c0, cw)

        def body(b):
            rs = rows_of(b)
            lifted = nn(n2[rs, :], wup[:, cs])
            half = 0.5 + 0.5 * lax.erf(lifted * (1.0 / math.sqrt(2.0)))
            act[rs, cs] = (lifted * half).astype(BF)
            slope = half + lifted * (jnp.exp(-0.5 * lifted * lifted) * (1.0 / math.sqrt(2.0 * math.pi)))
            glf[rs, cs] = (slope * nt(gl[rs, :], wdown[cs, :])).astype(BF)

        blocks(R // RB, body)

    def grad_tiles(c0, left, right, r0, cw):
        tile = 256 if cw % 256 == 0 else 128

        def body(j):
            off = pl.multiple_of(j * tile, tile)
            put(c0 + off, tile, nn(left, right[:, pl.ds(r0 + off, tile)]))

        blocks(cw // tile, body)

    steps = FF // plan.step
    for c in range(steps):
        c0 = c * plan.step
        feed(c0, plan.step)
        grad_tiles(c0, glt[...], act, c0, plan.step)
        made("down", c)
        service(1 if c == 0 else 2)
        grad_tiles(FF + c0, n2t[...], glf, c0, plan.step)
        made("up", c)
        service(1 if c == 0 else 2)

    swap_send = lambda i, t, src, dst: swap(i, t, src, dst).wait_send()
    for t in range(T):
        swap_send(0, t, xs, xr_a)
    for t in range(T):
        rows = pl.ds(t * S, S)

        def body(j, rows=rows):
            cs = pl.ds(pl.multiple_of(j * 256, 256), 256)
            xs[rows, cs] = nt(glf[rows, :], wup[cs, :]).astype(BF)
            ms[rows, cs] = nn(act[rows, :], wdown[:, cs]).astype(BF)

        blocks(D // 256, body)
        swap(1, t, xs, xr_b).start()
        swap(2, t, ms, mr).start()
        service(2)

    def output(b):
        rs = rows_of(b)
        pos = lax.broadcasted_iota(jnp.int32, (RB, 1), 0) + lax.rem(b * RB, S)
        live = pos < CTX + counts_ref[lax.div(b * RB, S)]
        total = resid[rs, :] + (ms[rs, :].astype(F32) + mr[rs, :].astype(F32))
        n2[rs, :] = jnp.where(live, total, 0.0).astype(BF)

    vec[...] = jnp.zeros_like(vec)

    def second_back(b):
        rs = rows_of(b)
        grad = xs[rs, :].astype(F32) + xr_b[rs, :].astype(F32)
        unit, inverse = unit_rows(resid[rs, :])
        vec[2:3, :] += jnp.sum(grad * unit, axis=0, keepdims=True)
        vec[3:4, :] += jnp.sum(grad, axis=0, keepdims=True)
        total = gl[rs, :].astype(F32) + norm_backward(grad, unit, inverse, g2)
        resid[rs, :] = total
        low = total.astype(BF)
        gl[rs, :] = low
        n2t[:, rs] = low.T

    for t in range(T):
        swap(2, t, ms, mr).wait_recv()
        blocks(per, lambda i, t=t: output(t * per + i))
        swap(1, t, xs, xr_b).wait_recv()
        blocks(per, lambda i, t=t: second_back(t * per + i))
        service(2)
    store_out = pltpu.make_async_copy(n2, out_hbm, out_sem.at[0])
    store_out.start()

    grad_tiles(plan.first["out"], n2t[...], ho, 0, H)
    made("out")
    service(2)

    gh, gq, gk, gv = 0, H, 2 * H, 3 * H

    def heads_back(t):
        rows = pl.ds(pl.multiple_of(t * S, S), S)
        act[rows, gh : gh + H] = nt(gl[rows, :], wout[...]).astype(BF)

    blocks(T, heads_back)
    service(2)

    def attend_back(t, h):
        rows = pl.ds(pl.multiple_of(t * S, S), S)
        context = pl.ds(pl.multiple_of(t * S, S), CTX)
        off = pl.multiple_of(h * PAIR, PAIR)
        cols = pl.ds(off, PAIR)
        slot = t * pairs + h
        grad2 = act[rows, pl.ds(gh + off, PAIR)]
        back = nt(stacked(v[context, cols]), grad2)
        low_p, low_s = [], []
        for i in range(2):
            p = prob[slot, i * CTX : (i + 1) * CTX, :]
            b = back[i * CTX : (i + 1) * CTX]
            low_p.append(p.astype(BF))
            low_s.append((p * (b - jnp.sum(p * b, axis=0, keepdims=True))).astype(BF))
        low_p = jnp.concatenate(low_p, axis=0)
        low_s = jnp.concatenate(low_s, axis=0)
        act[rows, pl.ds(gq + off, PAIR)] = (nn(beside(k[context, cols]), low_s).T * scale).astype(BF)
        act[context, pl.ds(gk + off, PAIR)] = (merged(nn(low_s, q[rows, cols])) * scale).astype(BF)
        act[context, pl.ds(gv + off, PAIR)] = merged(nn(low_p, grad2)).astype(BF)

    for t in range(T):
        blocks(pairs, lambda h, t=t: attend_back(t, h))
        service(2)

    def transpose_normed(b):
        rs = rows_of(b)
        glt[:, rs] = nrm[rs, :].T

    blocks(R // RB, transpose_normed)
    grad_tiles(plan.first["q"], glt[...], act, gq, H)
    made("q")
    service(2)

    def context_tiles(c0, r0):
        def body(j):
            off = pl.multiple_of(j * 128, 128)
            total = None
            for t in range(T):
                part = nn(glt[:, t * S : t * S + CTX], act[t * S : t * S + CTX, pl.ds(r0 + off, 128)])
                total = part if total is None else total + part
            put(c0 + off, 128, total)

        blocks(H // 128, body)

    context_tiles(plan.first["k"], gk)
    made("k")
    service(2)
    context_tiles(plan.first["v"], gv)
    made("v")
    service(2)

    for t in range(T):
        swap_send(1, t, xs, xr_b)
    for t in range(T):
        rows = pl.ds(t * S, S)

        def body(j, t=t, rows=rows):
            cs = pl.ds(pl.multiple_of(j * 256, 256), 256)
            part = nt(act[rows, gq : gq + H], wqkv[cs, 0:H])
            ctx = slice(t * S, t * S + CTX)
            extra = nt(act[ctx, gk : gk + 2 * H], wqkv[cs, H : 3 * H])
            xs[t * S : t * S + CTX, cs] = (part[:CTX] + extra).astype(BF)
            xs[t * S + CTX : (t + 1) * S, cs] = part[CTX:].astype(BF)

        blocks(D // 256, body)
        swap(3, t, xs, xr_a).start()
        service(1)

    def first_back(b):
        rs = rows_of(b)
        grad = xs[rs, :].astype(F32) + xr_a[rs, :].astype(F32)
        unit, inverse = unit_rows(x[rs, :].astype(F32))
        vec[0:1, :] += jnp.sum(grad * unit, axis=0, keepdims=True)
        vec[1:2, :] += jnp.sum(grad, axis=0, keepdims=True)
        resid[rs, :] = resid[rs, :] + norm_backward(grad, unit, inverse, g1)

    for t in range(T):
        swap(3, t, xs, xr_a).wait_recv()
        blocks(per, lambda i, t=t: first_back(t * per + i))
    store_gin = pltpu.make_async_copy(resid, gin_hbm, out_sem.at[1])
    store_gin.start()
    put(plan.first["vec"], 128, jnp.concatenate([vec[...], jnp.zeros((128 - vec.shape[0], D), F32)], axis=0).T)
    made("vec")
    service(1000)
    assert not events

    if plan.fused:
        store_red = pltpu.make_async_copy(red, red_hbm, out_sem.at[2])
    else:
        store_red = pltpu.make_async_copy(g, red_hbm, out_sem.at[2])
    store_red.start()
    if plan.fused:
        for p in prog:
            p[4]()
    for t in range(T):
        swap_send(2, t, ms, mr)
        swap_send(3, t, xs, xr_a)
    store_out.wait()
    store_gin.wait()
    store_red.wait()


def run_layer(plan, counts, x, wqkv, wout, wup, wdown, gains, cot):
    R, D, H, FF, W = plan.rows, plan.width, plan.heads, plan.hidden, plan.columns
    V = pltpu.VMEM
    DMA = pltpu.SemaphoreType.DMA
    n = len(plan.chunks)
    if plan.fused:
        gshape, redshape, share = (4, 2, 2, plan.share, W), (plan.share, W), plan.share
        comm = [V((4, 2, share, W), BF), V((4, share, W), BF), V((3, share, W), BF), V(redshape, F32)]
        red_type = jax.ShapeDtypeStruct(redshape, F32)
    else:
        gshape = (D, W)
        comm = [V((8, 128), F32)] * 4
        red_type = jax.ShapeDtypeStruct(gshape, BF)
    scratch = [
        V((R, D), BF), V((D, 3 * H), BF), V((H, D), BF), V((D, FF), BF), V((FF, D), BF), V((4, D), F32), V((R, D), BF),
        V((R, D), BF), V((R, H), BF), V((R, H), BF), V((R, H), BF),
        V((plan.tables * (H // PAIR), 2 * CTX, plan.seq), F32), V((R, H), BF), V((R, D), F32), V((R, D), BF),
        V((D, R), BF), V((D, R), BF), V((R, FF), BF), V((R, FF), BF), V((8, D), F32),
        V((R, D), BF), V((R, D), BF), V((R, D), BF), V((R, D), BF), V((R, D), BF),
        V(gshape, BF), *comm,
        DMA((7,)), DMA((3,)), DMA((4, plan.tables)), DMA((4, plan.tables)),
        DMA((n,)), DMA((n,)), DMA((n,)), DMA((n,)), DMA((n, 3)), DMA((n, 3)),
    ]
    hbm = pl.BlockSpec(memory_space=pl.ANY)

    def kernel(*refs):
        layer_kernel(plan, *refs)

    return pl.pallas_call(
        kernel,
        out_shape=(jax.ShapeDtypeStruct((R, D), BF), jax.ShapeDtypeStruct((R, D), F32), red_type),
        in_specs=[pl.BlockSpec(memory_space=pltpu.SMEM)] + [hbm] * 7,
        out_specs=(hbm,) * 3,
        scratch_shapes=scratch,
        compiler_params=pltpu.CompilerParams(collective_id=0, has_side_effects=True, vmem_limit_bytes=67043328),
        name="layer",
    )(counts, x, wqkv, wout, wup, wdown, gains, cot)


def per_device(dp, inputs, counts, w_qkv, w_out, w_up, w_down, gain_one, shift_one, gain_two, shift_two, cotangent):
    tables, seq, width = inputs.shape
    heads, hidden = w_out.shape[0], w_up.shape[1]
    plan = Plan(tables, seq, width, heads, hidden, dp)
    rows = tables * seq
    out, gin, red = run_layer(
        plan,
        counts,
        inputs.reshape(rows, width),
        w_qkv.reshape(width, 3 * heads),
        w_out,
        w_up,
        w_down,
        jnp.stack([gain_one, shift_one, gain_two, shift_two]),
        cotangent.reshape(rows, width),
    )
    if not plan.fused:
        red = lax.psum_scatter(red.astype(F32), "dp", scatter_dimension=0, tiled=True)
    at = 2 * hidden
    vec = red[:, at + 4 * heads : at + 4 * heads + 4]
    return (
        out.reshape(inputs.shape),
        gin.reshape(inputs.shape),
        red[:, at + heads : at + 4 * heads].reshape(-1, 3, heads),
        red[:, at : at + heads].T,
        red[:, hidden:at],
        red[:, :hidden].T,
        vec[:, 0],
        vec[:, 1],
        vec[:, 2],
        vec[:, 3],
    )


def solution(mesh):
    dp = mesh.shape["dp"]
    in_specs = (
        P("dp", None, None), P("dp"), P(None, None, "mp"), P("mp", None), P(None, "mp"), P("mp", None),
        P(), P(), P(), P(), P("dp", None, None),
    )
    out_specs = (
        P("dp", None, None), P("dp", None, None), P("dp", None, "mp"), P("mp", "dp"), P("dp", "mp"), P("mp", "dp"),
        P("dp"), P("dp"), P("dp"), P("dp"),
    )

    def step(*args):
        return per_device(dp, *args)

    return jax.shard_map(step, mesh=mesh, in_specs=in_specs, out_specs=out_specs, check_vma=False)
```

```python
import math

import jax
import jax.numpy as jnp
from jax import lax
from jax.experimental import pallas as pl
from jax.experimental.pallas import tpu as pltpu
from jax.sharding import PartitionSpec as P

HD = 64
CTX = 384
EPS = 1e-05
BF = jnp.bfloat16
F32 = jnp.float32
MESH = pl.DeviceIdType.MESH
PAIR = 2 * HD
RB = 256


def nn(a, b):
    return lax.dot_general(a, b, (((1,), (0,)), ((), ())), preferred_element_type=F32)


def nt(a, b):
    return lax.dot_general(a, b, (((1,), (1,)), ((), ())), preferred_element_type=F32)


def unit_rows(rows):
    centre = jnp.mean(rows, axis=-1, keepdims=True)
    centred = rows - centre
    inverse = lax.rsqrt(jnp.mean(centred * centred, axis=-1, keepdims=True) + EPS)
    return centred * inverse, inverse


def norm_backward(grad, unit, inverse, gain):
    u = grad * gain
    first = jnp.mean(u, axis=-1, keepdims=True)
    second = jnp.mean(u * unit, axis=-1, keepdims=True)
    return inverse * (u - first - unit * second)


HOPS = ('x', 'y', 'x', 'y', 'zy', 'x', 'x', 'x', 'y', 'zy', 'zy', 'y', 'x', 'x', 'y', 'y', 'x', 'y', 'y', 'x', 'y', 'x', 'y', 'x', 'x')
ORDER = ((0, 0), (1, 0), (2, 0), (3, 0), (4, 0), (5, 0), (0, 1), (1, 1), (2, 1), (8, 0), (3, 1), (4, 1), (9, 0), (0, 2), (6, 0), (5, 1), (2, 2), (11, 0), (1, 2), (7, 0), (3, 2), (8, 1), (9, 1), (4, 2), (5, 2), (6, 1), (14, 0), (12, 0), (0, 3), (11, 1), (10, 0), (4, 3), (7, 1), (9, 2), (6, 2), (8, 2), (13, 0), (14, 1), (12, 1), (2, 3), (7, 2), (11, 2), (15, 0), (16, 0), (4, 4), (1, 3), (9, 3), (17, 0), (3, 3), (10, 1), (19, 0), (18, 0), (5, 3), (12, 2), (13, 1), (14, 2), (21, 0), (15, 1), (20, 0), (16, 1), (9, 4), (6, 3), (17, 1), (23, 0), (22, 0), (19, 1), (18, 1), (13, 2), (10, 2), (21, 1), (8, 3), (15, 2), (7, 3), (17, 2), (16, 2), (20, 1), (11, 3), (12, 3), (23, 1), (24, 0), (14, 3), (22, 1), (18, 2), (13, 3), (19, 2), (20, 2), (15, 3), (10, 3), (21, 2), (17, 3), (24, 1), (23, 2), (16, 3), (22, 2), (10, 4), (18, 3), (19, 3), (24, 2), (20, 3), (21, 3), (23, 3), (22, 3), (24, 3))
SERVE = (1, 2, 3, 4, 5, 6, 8, 8, 11, 13, 15, 16, 17, 19, 19, 20, 21, 24, 25, 26, 26, 28, 31, 33, 33, 37, 38, 39, 48, 52, 55, 57, 59, 60, 63, 65, 67, 67, 70, 72, 76, 77, 82, 83, 86, 88, 89, 90)


class Plan:
    def __init__(self, tables, seq, width, heads, hidden, dp):
        self.tables, self.seq, self.width, self.heads, self.hidden, self.dp = tables, seq, width, heads, hidden, dp
        self.rows = tables * seq
        self.share = width // dp
        self.fused = dp == 16 and self.share % 16 == 0
        self.step = 256
        steps = hidden // self.step
        chunks = []
        self.z_columns = 0
        self.z_at = []
        for c in range(steps):
            for name, at in (("down", 0), ("up", hidden)):
                chunks.append((name, at + c * self.step, self.step))
        at = 2 * hidden
        self.first = {"down": 0, "up": hidden}
        self.piece = 128
        for name in ("out", "q", "k", "v"):
            self.first[name] = at
            for j in range(heads // self.piece):
                chunks.append((name, at, self.piece))
                at += self.piece
        self.first["vec"] = at
        chunks.append(("vec", at, 128))
        chunks = [c + (HOPS[i % len(HOPS)],) for i, c in enumerate(chunks)]
        for _, _, cw, kind in chunks:
            self.z_at.append(self.z_columns)
            self.z_columns += cw if kind[0] == "z" else 0
        self.chunks = chunks
        self.columns = at + 128
        self.finish_parts = (8, 4, 1, 1, 1, 1)
        if self.fused:
            shapes = ((self.share, hidden), (self.share, hidden), (self.share, heads), (3, self.share, heads), (8, self.share))
            self.grad_shapes = tuple((a, F32) for a in shapes)
        else:
            self.grad_shapes = (((width, self.columns), BF),)


def layer_kernel(
    plan,
    counts_ref, x_hbm, wqkv_hbm, wout_hbm, wup_hbm, wdown_hbm, cot_hbm, g1_ref, b1_ref, g2_ref, b2_ref,
    out_hbm, gin_hbm, *rest,
):
    grads_hbm, rest = rest[: len(plan.grad_shapes)], rest[len(plan.grad_shapes) :]
    (
        x, wqkv, wout, wup, wdown, gl,
    nrm, q, k, v, prob, ho, resid, gres, n2, n2t, glt, act, glf, vec,
    xs, xr_a, xr_b, mr,
    g, r1, r2, r3, r4, red, vecs,
    in_sem, out_sem, red_sem, xsend, xrecv, send, recv,
    ) = rest
    T, S, D, H, FF = plan.tables, plan.seq, plan.width, plan.heads, plan.hidden
    R = plan.rows
    pairs = H // PAIR
    dp = lax.axis_index("dp")
    mp = lax.axis_index("mp")
    xx, yy, zz = lax.rem(dp, 2), lax.rem(lax.div(dp, 2), 2), lax.div(dp, 4)
    partner = (dp, 1 - mp)

    def chip(z, y, x_):
        return (z * 4 + y * 2 + x_, mp)

    x_peer, y_peer = chip(zz, yy, 1 - xx), chip(zz, 1 - yy, xx)
    z_peers = [chip(lax.rem(zz + d, 4), yy, xx) for d in (1, 2, 3)]
    peers = [partner] + ([x_peer, y_peer] + z_peers if plan.fused else [])

    loads = [
        pltpu.make_async_copy(a, b, in_sem.at[i])
        for i, (a, b) in enumerate(
            ((x_hbm, x), (wqkv_hbm, wqkv), (wout_hbm, wout), (cot_hbm, gl), (wup_hbm, wup), (wdown_hbm, wdown))
        )
    ]
    for c in loads:
        c.start()
    barrier = pltpu.get_barrier_semaphore()
    for n in peers:
        pl.semaphore_signal(barrier, inc=1, device_id=n, device_id_type=MESH)
    pl.semaphore_wait(barrier, len(peers))

    def remote(src, dst, ss, rs, dev):
        return pltpu.make_async_remote_copy(src, dst, ss, rs, device_id=dev, device_id_type=MESH)

    def swap(i, t, src, dst):
        rows = pl.ds(t * S, S)
        return remote(src.at[rows], dst.at[rows], xsend.at[i, t], xrecv.at[i, t], partner)

    zh, zl = lax.div(zz, 2), lax.rem(zz, 2)
    outer = lax.rem(zh + zl + 1, 2)

    stores = {}

    def store(i):
        name, c0, cw, _ = plan.chunks[i]
        off = c0 - plan.first[name]
        if name == "vec":
            vecs[...] = red[:, c0 : c0 + cw].T
            stores[i] = pltpu.make_async_copy(vecs.at[0:8], grads_hbm[4], red_sem.at[i])
        else:
            at = {"down": 0, "up": 1, "out": 2, "q": 3, "k": 3, "v": 3}[name]
            dst = grads_hbm[at].at["qkv".index(name)] if at == 3 else grads_hbm[at]
            stores[i] = pltpu.make_async_copy(red.at[:, pl.ds(c0, cw)], dst.at[:, pl.ds(off, cw)], red_sem.at[i])
        stores[i].start()

    def add(dst, a, b):
        dst[...] = (a[...].astype(F32) + b[...].astype(F32)).astype(BF)

    def flat(i):
        _, c0, cw, kind = plan.chunks[i]
        cs = pl.ds(c0, cw)
        isx = kind == "x"
        other, mine = (1 - yy, yy) if isx else (1 - xx, xx)
        c1 = remote(
            g.at[:, :, :, 1 - xx, :, cs] if isx else g.at[:, :, 1 - yy, :, :, cs],
            r1.at[:, :, :, :, cs], send.at[i, 0], recv.at[i, 0], x_peer if isx else y_peer,
        )
        c2 = remote(r1.at[:, :, other, :, cs], r2.at[:, :, :, cs], send.at[i, 1], recv.at[i, 1], y_peer if isx else x_peer)
        c3 = []
        for d in (1, 2, 3):
            z = lax.rem(zz + d, 4)
            c3.append(
                remote(r2.at[lax.div(z, 2), lax.rem(z, 2), :, cs], r3.at[d - 1, :, cs], send.at[i, 1 + d], recv.at[i, 1 + d], z_peers[d - 1])
            )

        def add_one():
            c1.wait_recv()

            def part(p):
                for h in range(2):
                    for l in range(2):
                        own = g.at[h, l, p, xx, :, cs] if isx else g.at[h, l, yy, p, :, cs]
                        add(r1.at[h, l, p, :, cs], own, r1.at[h, l, p, :, cs])

            part(other)
            c2.start()
            part(mine)

        def add_two():
            c2.wait_recv()
            for d in (2, 3, 1, 0):
                z = lax.rem(zz + d, 4)
                h, l = lax.div(z, 2), lax.rem(z, 2)
                add(r2.at[h, l, :, cs], r1.at[h, l, mine, :, cs], r2.at[h, l, :, cs])
                if d:
                    c3[d - 1].start()

        def add_three():
            for c in c3:
                c.wait_recv()
            total = r2[zh, zl, :, cs].astype(F32)
            for d in range(3):
                total = total + r3[d, :, cs].astype(F32)
            red[:, cs] = total
            store(i)

        def drain():
            for c in (c1, c2, *c3):
                c.wait_send()

        return [c1.start, add_one, add_two, add_three], drain

    def upright(i):
        _, c0, cw, kind = plan.chunks[i]
        cs, zs = pl.ds(c0, cw), pl.ds(plan.z_at[i], cw)
        isx = kind == "zx"
        kept = jnp.where(outer == 1, zh, 1 - zh)
        mate = chip(zh * 2 + 1 - zl, yy, xx)
        across_mid = chip(3 - zz, yy, xx)
        across_end = chip((1 - zh) * 3, yy, xx)
        ca = remote(g.at[1 - kept, :, :, :, :, cs], r1.at[:, :, :, :, cs], send.at[i, 0], recv.at[i, 0], mate)
        end_b = remote(r1.at[1 - zl, :, :, :, cs], r4.at[:, :, :, zs], send.at[i, 1], recv.at[i, 1], mate)
        mid_b = remote(r1.at[1 - zl, :, :, :, cs], r2.at[:, :, :, cs], send.at[i, 1], recv.at[i, 2], across_mid)
        far_b = remote(r1.at[zl, :, :, :, cs], r2.at[:, :, :, cs], send.at[i, 2], recv.at[i, 2], across_end)
        if isx:
            half, single = r2.at[:, 1 - xx, :, cs], r2.at[1 - yy, xx, :, cs]
        else:
            half, single = r2.at[1 - yy, :, :, cs], r2.at[yy, 1 - xx, :, cs]
        cc = remote(half, r3.at[0:2, :, cs], send.at[i, 3], recv.at[i, 3], x_peer if isx else y_peer)
        cd = remote(single, r3.at[2, :, cs], send.at[i, 4], recv.at[i, 4], y_peer if isx else x_peer)

        def add_one():
            ca.wait_recv()
            for l in range(2):
                for y in range(2):
                    for x_ in range(2):
                        add(r1.at[l, y, x_, :, cs], g.at[kept, l, y, x_, :, cs], r1.at[l, y, x_, :, cs])

            @pl.when(outer == 1)
            def _():
                end_b.start()

            @pl.when(outer == 0)
            def _():
                mid_b.start()
                far_b.start()

        def add_two():
            mid_b.wait_recv()

            @pl.when(outer == 0)
            def _():
                end_b.wait_recv()

            def part(y, x_):
                @pl.when(outer == 1)
                def _():
                    add(r2.at[y, x_, :, cs], r1.at[zl, y, x_, :, cs], r2.at[y, x_, :, cs])

                @pl.when(outer == 0)
                def _():
                    add(r2.at[y, x_, :, cs], r4.at[y, x_, :, zs], r2.at[y, x_, :, cs])

            for p in range(2):
                part(p, 1 - xx) if isx else part(1 - yy, p)
            cc.start()
            for p in range(2):
                part(p, xx) if isx else part(yy, p)

        def add_three():
            cc.wait_recv()

            def part(p):
                at = r2.at[p, xx, :, cs] if isx else r2.at[yy, p, :, cs]
                add(at, at, r3.at[p, :, cs])

            other, mine = (1 - yy, yy) if isx else (1 - xx, xx)
            part(other)
            cd.start()
            part(mine)

        def add_four():
            cd.wait_recv()
            red[:, cs] = r2[yy, xx, :, cs].astype(F32) + r3[2, :, cs].astype(F32)
            store(i)

        def drain():
            ca.wait_send()

            @pl.when(outer == 1)
            def _():
                end_b.wait_send()

            @pl.when(outer == 0)
            def _():
                mid_b.wait_send()
                far_b.wait_send()

            cc.wait_send()
            cd.wait_send()

        return [ca.start, add_one, add_two, add_three, add_four], drain

    ready = set()
    events = []
    prog = []
    if plan.fused:
        prog = [upright(i) if c[3][0] == "z" else flat(i) for i, c in enumerate(plan.chunks)]
        events = list(ORDER)

    served = [0]

    def service(everything=False):
        limit = len(ORDER) if everything or served[0] >= len(SERVE) else SERVE[served[0]]
        served[0] += 1
        while events and len(ORDER) - len(events) < limit and events[0][0] in ready:
            i, stage = events.pop(0)
            prog[i][0][stage]()

    def made(name, c0, cw):
        for j, c in enumerate(plan.chunks):
            if c0 <= c[1] < c0 + cw:
                ready.add(j)

    def put(c0, cw, rows768):
        cs = pl.ds(c0, cw)
        if plan.fused:
            g[:, :, :, :, :, cs] = rows768.astype(BF).reshape(2, 2, 2, 2, plan.share, cw)
        else:
            g[:, cs] = rows768.astype(BF)

    def blocks(n, body):
        def step(i, carry):
            body(i)
            return carry

        lax.fori_loop(0, n, step, 0)

    def rows_of(b):
        return pl.ds(pl.multiple_of(b * RB, RB), RB)

    loads[0].wait()
    g1, b1, g2, b2 = (a[...].reshape(1, D) for a in (g1_ref, b1_ref, g2_ref, b2_ref))

    def first_norm(b):
        rs = rows_of(b)
        unit, _ = unit_rows(x[rs, :].astype(F32))
        nrm[rs, :] = (unit * g1 + b1).astype(BF)

    blocks(R // RB, first_norm)
    loads[1].wait()

    def project(t):
        all_rows = pl.ds(pl.multiple_of(t * S, S), S)
        context = pl.ds(pl.multiple_of(t * S, S), CTX)
        q[all_rows, :] = nn(nrm[all_rows, :], wqkv[0]).astype(BF)
        kept = pl.ds(pl.multiple_of(t * CTX, CTX), CTX)
        k[kept, :] = nn(nrm[context, :], wqkv[1]).astype(BF)
        v[kept, :] = nn(nrm[context, :], wqkv[2]).astype(BF)

    blocks(T, project)

    scale = 1.0 / math.sqrt(HD)
    low_lane = lax.broadcasted_iota(jnp.int32, (CTX, PAIR), 1) < HD
    low_row = lax.broadcasted_iota(jnp.int32, (PAIR, CTX), 0) < HD

    def stacked(a):
        zero = jnp.zeros_like(a)
        return jnp.concatenate([jnp.where(low_lane, a, zero), jnp.where(low_lane, zero, a)], axis=0)

    def beside(a):
        at = a.T
        zero = jnp.zeros_like(at)
        return jnp.concatenate([jnp.where(low_row, at, zero), jnp.where(low_row, zero, at)], axis=1)

    def merged(a):
        return jnp.where(low_lane, a[:CTX], a[CTX:])

    def attend(t, h):
        rows = pl.ds(pl.multiple_of(t * S, S), S)
        kept = pl.ds(pl.multiple_of(t * CTX, CTX), CTX)
        cols = pl.ds(pl.multiple_of(h * PAIR, PAIR), PAIR)
        slot = t * pairs + h
        scores = nt(stacked(k[kept, cols]), q[rows, cols])
        halves = []
        for i in range(2):
            s = scores[i * CTX : (i + 1) * CTX]
            e = jnp.exp((s - jnp.max(s, axis=0, keepdims=True)) * scale)
            p = e * (1.0 / jnp.sum(e, axis=0, keepdims=True))
            prob[slot, i * CTX : (i + 1) * CTX, :] = p
            halves.append(p.astype(BF))
        out_t = nn(beside(v[kept, cols]), jnp.concatenate(halves, axis=0))
        ho[rows, cols] = out_t.T.astype(BF)

    loads[2].wait()
    for t in range(T):
        blocks(pairs, lambda h, t=t: attend(t, h))
        rows = pl.ds(t * S, S)
        xs[rows, :] = nn(ho[rows, :], wout[...]).astype(BF)
        swap(0, t, xs, xr_a).start()

    loads[3].wait()

    def mask(b):
        rs = rows_of(b)
        pos = lax.broadcasted_iota(jnp.int32, (RB, 1), 0) + lax.rem(b * RB, S)
        live = pos < CTX + counts_ref[lax.div(b * RB, S)]
        kept = jnp.where(live, gl[rs, :].astype(F32), 0.0).astype(BF)
        gl[rs, :] = kept
        glt[:, rs] = kept.T

    blocks(R // RB, mask)

    def second_norm(b):
        rs = rows_of(b)
        r = x[rs, :].astype(F32) + (xs[rs, :].astype(F32) + xr_a[rs, :].astype(F32))
        resid[rs, :] = r
        unit, _ = unit_rows(r)
        low = (unit * g2 + b2).astype(BF)
        n2[rs, :] = low
        n2t[:, rs] = low.T

    per = S // RB
    for t in range(T):
        swap(0, t, xs, xr_a).wait_recv()
        blocks(per, lambda i, t=t: second_norm(t * per + i))
    loads[4].wait()
    loads[5].wait()

    def feed(c0, cw):
        cs = pl.ds(c0, cw)

        def body(b):
            rs = rows_of(b)
            lifted = nn(n2[rs, :], wup[:, cs])
            half = 0.5 + 0.5 * lax.erf(lifted * (1.0 / math.sqrt(2.0)))
            act[rs, cs] = (lifted * half).astype(BF)
            slope = half + lifted * (jnp.exp(-0.5 * lifted * lifted) * (1.0 / math.sqrt(2.0 * math.pi)))
            glf[rs, cs] = (slope * nt(gl[rs, :], wdown[cs, :])).astype(BF)

        blocks(R // RB, body)

    def grad(name, c0, left, right, r0, cw):
        at = plan.first[name] + c0
        put(at, cw, nn(left, right[:, r0 : r0 + cw]))
        made(name, at, cw)

    for c in range(FF // plan.step):
        c0 = c * plan.step
        feed(c0, plan.step)
        grad("down", c0, glt[...], act, c0, plan.step)
        service()
        grad("up", c0, n2t[...], glf, c0, plan.step)
        service()

    for t in range(T):
        swap(0, t, xs, xr_a).wait_send()
    for t in range(T):
        rows = pl.ds(t * S, S)
        for j in range(D // 256):
            xs[rows, j * 256 : (j + 1) * 256] = nt(glf[rows, :], wup[j * 256 : (j + 1) * 256, :]).astype(BF)
            service()
        swap(1, t, xs, xr_b).start()

    vec[...] = jnp.zeros_like(vec)

    def second_back(b):
        rs = rows_of(b)
        grad_norm = xs[rs, :].astype(F32) + xr_b[rs, :].astype(F32)
        unit, inverse = unit_rows(resid[rs, :])
        vec[2:3, :] += jnp.sum(grad_norm * unit, axis=0, keepdims=True)
        vec[3:4, :] += jnp.sum(grad_norm, axis=0, keepdims=True)
        total = gl[rs, :].astype(F32) + norm_backward(grad_norm, unit, inverse, g2)
        gres[rs, :] = total
        low = total.astype(BF)
        gl[rs, :] = low
        n2t[:, rs] = low.T

    for t in range(T):
        swap(1, t, xs, xr_b).wait_recv()
        blocks(per, lambda i, t=t: second_back(t * per + i))
        service()

    gh, gq, gk, gv = 0, H, 2 * H, 3 * H
    for t in range(T):
        rows = slice(t * S, (t + 1) * S)
        glf[rows, gh : gh + H] = nt(gl[rows, :], wout[...]).astype(BF)
    service()
    grad("out", 0, n2t[...], ho, 0, H)
    service()

    def attend_back(t, h):
        rows = pl.ds(pl.multiple_of(t * S, S), S)
        context = pl.ds(pl.multiple_of(t * S, S), CTX)
        kept = pl.ds(pl.multiple_of(t * CTX, CTX), CTX)
        off = pl.multiple_of(h * PAIR, PAIR)
        cols = pl.ds(off, PAIR)
        slot = t * pairs + h
        grad2 = glf[rows, pl.ds(gh + off, PAIR)]
        back = nt(stacked(v[kept, cols]), grad2)
        low_p, low_s = [], []
        for i in range(2):
            p = prob[slot, i * CTX : (i + 1) * CTX, :]
            b = back[i * CTX : (i + 1) * CTX]
            low_p.append(p.astype(BF))
            low_s.append((p * (b - jnp.sum(p * b, axis=0, keepdims=True))).astype(BF))
        low_p = jnp.concatenate(low_p, axis=0)
        low_s = jnp.concatenate(low_s, axis=0)
        glf[rows, pl.ds(gq + off, PAIR)] = (nn(beside(k[kept, cols]), low_s).T * scale).astype(BF)
        glf[context, pl.ds(gk + off, PAIR)] = (merged(nn(low_s, q[rows, cols])) * scale).astype(BF)
        glf[context, pl.ds(gv + off, PAIR)] = merged(nn(low_p, grad2)).astype(BF)

    for t in range(T):
        for h in range(pairs):
            attend_back(t, h)
            service()

    def transpose_normed(b):
        rs = rows_of(b)
        glt[:, rs] = nrm[rs, :].T

    blocks(R // RB, transpose_normed)
    grad("q", 0, glt[...], glf, gq, H)
    service()

    def grad_context(name, r0):
        total = None
        for t in range(T):
            part = nn(glt[:, t * S : t * S + CTX], glf[t * S : t * S + CTX, r0 : r0 + H])
            total = part if total is None else total + part
        put(plan.first[name], H, total)
        made(name, plan.first[name], H)
        service()

    grad_context("k", gk)
    grad_context("v", gv)

    for t in range(T):
        swap(1, t, xs, xr_b).wait_send()
    for t in range(T):
        rows = slice(t * S, (t + 1) * S)
        ctx = slice(t * S, t * S + CTX)
        for j in range(D // 256):
            cs = slice(j * 256, (j + 1) * 256)
            part = nt(glf[rows, gq : gq + H], wqkv[0, cs, :])
            extra = nt(glf[ctx, gk : gk + H], wqkv[1, cs, :]) + nt(glf[ctx, gv : gv + H], wqkv[2, cs, :])
            xs[ctx, cs] = (part[:CTX] + extra).astype(BF)
            xs[t * S + CTX : (t + 1) * S, cs] = part[CTX:].astype(BF)
            service()
        swap(3, t, xs, xr_a).start()

    def feed_out(t):
        rows = slice(t * S, (t + 1) * S)
        for j in range(D // 256):
            cs = slice(j * 256, (j + 1) * 256)
            nrm[rows, cs] = nn(act[rows, :], wdown[:, cs]).astype(BF)
            service()
        swap(2, t, nrm, mr).start()

    feed_out(0)

    def first_back(b):
        rs = rows_of(b)
        grad_norm = xs[rs, :].astype(F32) + xr_a[rs, :].astype(F32)
        unit, inverse = unit_rows(x[rs, :].astype(F32))
        vec[0:1, :] += jnp.sum(grad_norm * unit, axis=0, keepdims=True)
        vec[1:2, :] += jnp.sum(grad_norm, axis=0, keepdims=True)
        gres[rs, :] = gres[rs, :] + norm_backward(grad_norm, unit, inverse, g1)

    for t in range(T):
        swap(3, t, xs, xr_a).wait_recv()
        blocks(per, lambda i, t=t: first_back(t * per + i))
        service()
    store_gin = pltpu.make_async_copy(gres, gin_hbm, out_sem.at[1])
    store_gin.start()
    put(plan.first["vec"], 128, jnp.concatenate([vec[...], jnp.zeros((128 - vec.shape[0], D), F32)], axis=0).T)
    made("vec", plan.first["vec"], 128)
    service()

    for t in range(1, T):
        feed_out(t)

    def output(b):
        rs = rows_of(b)
        pos = lax.broadcasted_iota(jnp.int32, (RB, 1), 0) + lax.rem(b * RB, S)
        live = pos < CTX + counts_ref[lax.div(b * RB, S)]
        total = resid[rs, :] + (nrm[rs, :].astype(F32) + mr[rs, :].astype(F32))
        n2[rs, :] = jnp.where(live, total, 0.0).astype(BF)

    for t in range(T):
        swap(2, t, nrm, mr).wait_recv()
        blocks(per, lambda i, t=t: output(t * per + i))
        service()
    store_out = pltpu.make_async_copy(n2, out_hbm, out_sem.at[0])
    store_out.start()
    service(True)
    assert not events

    if not plan.fused:
        stores[0] = pltpu.make_async_copy(g, grads_hbm[0], red_sem.at[0])
        stores[0].start()
    for p in prog:
        p[1]()
    for t in range(T):
        swap(2, t, nrm, mr).wait_send()
        swap(3, t, xs, xr_a).wait_send()
    store_out.wait()
    store_gin.wait()
    for c in stores.values():
        c.wait()


def run_layer(plan, counts, x, wqkv, wout, wup, wdown, cot, gains):
    R, D, H, FF, W = plan.rows, plan.width, plan.heads, plan.hidden, plan.columns
    V = pltpu.VMEM
    DMA = pltpu.SemaphoreType.DMA
    n = len(plan.chunks)
    share = plan.share
    if plan.fused:
        gshape = (2, 2, 2, 2, share, W)
        comm = [V((2, 2, 2, share, W), BF), V((2, 2, share, W), BF), V((3, share, W), BF)]
        comm += [V((2, 2, share, plan.z_columns), BF), V((share, W), F32), V((128, share), F32)]
    else:
        gshape = (D, W)
        comm = [V((8, 128), F32)] * 6
    scratch = [
        V((R, D), BF), V((3, D, H), BF), V((H, D), BF), V((D, FF), BF), V((FF, D), BF), V((R, D), BF),
        V((R, D), BF), V((R, H), BF), V((plan.tables * CTX, H), BF), V((plan.tables * CTX, H), BF),
        V((plan.tables * (H // PAIR), 2 * CTX, plan.seq), F32), V((R, H), BF), V((R, D), F32), V((R, D), F32), V((R, D), BF),
        V((D, R), BF), V((D, R), BF), V((R, FF), BF), V((R, FF), BF), V((8, D), F32),
        V((R, D), BF), V((R, D), BF), V((R, D), BF), V((R, D), BF),
        V(gshape, BF), *comm,
        DMA((6,)), DMA((2,)), DMA((n,)), DMA((4, plan.tables)), DMA((4, plan.tables)),
        DMA((n, 5)), DMA((n, 5)),
    ]
    hbm = pl.BlockSpec(memory_space=pl.ANY)

    def kernel(*refs):
        layer_kernel(plan, *refs)

    return pl.pallas_call(
        kernel,
        out_shape=(
            jax.ShapeDtypeStruct((R, D), BF),
            jax.ShapeDtypeStruct((R, D), F32),
            *(jax.ShapeDtypeStruct(*a) for a in plan.grad_shapes),
        ),
        in_specs=[pl.BlockSpec(memory_space=pltpu.SMEM)] + [hbm] * 6 + [pl.BlockSpec(memory_space=pltpu.VMEM)] * 4,
        out_specs=(hbm,) * (2 + len(plan.grad_shapes)),
        scratch_shapes=scratch,
        compiler_params=pltpu.CompilerParams(collective_id=0, has_side_effects=True, vmem_limit_bytes=67043328),
        name="layer",
    )(counts, x, wqkv, wout, wup, wdown, cot, *gains)


def finish_kernel(plan, *refs):
    n = 6
    src, vec_ref, dst, vec_out = refs[:n], refs[n], refs[n + 1 : 2 * n + 1], refs[2 * n + 1 : 2 * n + 5]
    bufs, in_sem, out_sem = refs[2 * n + 5 : 3 * n + 5], refs[3 * n + 5], refs[3 * n + 6]
    moves = []
    for i in range(n):
        rows = src[i].shape[0]
        parts = plan.finish_parts[i]
        for j in range(parts):
            moves.append((i, pl.ds(j * (rows // parts), rows // parts)))
    loads, stores = [], []
    for m, (i, rows) in enumerate(moves):
        loads.append(pltpu.make_async_copy(src[i].at[rows], bufs[i].at[rows], in_sem.at[m]))
        stores.append(pltpu.make_async_copy(bufs[i].at[rows], dst[i].at[rows], out_sem.at[m]))
    for c in loads:
        c.start()
    for i in range(4):
        vec_out[i][...] = vec_ref[i, :]
    for a, b in zip(loads, stores):
        a.wait()
        b.start()
    for c in stores:
        c.wait()


def finish(plan, shape, out, gin, down, up, o, qkv, vec):
    arrays = (gin, out, up, down, qkv, o)
    n = sum(plan.finish_parts)
    hbm = pl.BlockSpec(memory_space=pltpu.HBM)
    vmem = pl.BlockSpec(memory_space=pltpu.VMEM)
    share = plan.share

    def kernel(*refs):
        finish_kernel(plan, *refs)

    gin, out, up, down, qkv, o, *norms = pl.pallas_call(
        kernel,
        out_shape=tuple(jax.ShapeDtypeStruct(a.shape, a.dtype) for a in arrays)
        + tuple(jax.ShapeDtypeStruct((share,), F32) for _ in range(4)),
        in_specs=[hbm] * 6 + [vmem],
        out_specs=(hbm,) * 6 + (vmem,) * 4,
        scratch_shapes=[pltpu.VMEM(a.shape, a.dtype) for a in arrays]
        + [pltpu.SemaphoreType.DMA((n,)), pltpu.SemaphoreType.DMA((n,))],
        name="finish",
    )(*arrays, vec)
    return (out.reshape(shape), gin.reshape(shape), jnp.transpose(qkv, (1, 0, 2)), o.T, up, down.T, *norms)


def per_device(dp, inputs, counts, w_qkv, w_out, w_up, w_down, gain_one, shift_one, gain_two, shift_two, cotangent):
    tables, seq, width = inputs.shape
    heads, hidden = w_out.shape[0], w_up.shape[1]
    plan = Plan(tables, seq, width, heads, hidden, dp)
    rows = tables * seq
    gains = (gain_one, shift_one, gain_two, shift_two)
    out, gin, *grads = run_layer(
        plan,
        counts,
        inputs.reshape(rows, width),
        jnp.transpose(w_qkv, (1, 0, 2)),
        w_out,
        w_up,
        w_down,
        cotangent.reshape(rows, width),
        gains,
    )
    if plan.fused:
        down, up, o, qkv, vec = grads
        return finish(plan, inputs.shape, out, gin, down, up, o, qkv, vec)
    else:
        red = lax.psum_scatter(grads[0].astype(F32), "dp", scatter_dimension=0, tiled=True)
        at = 2 * hidden
        down, up, o = red[:, :hidden], red[:, hidden:at], red[:, at : at + heads]
        qkv = red[:, at + heads : at + 4 * heads].reshape(-1, 3, heads).transpose(1, 0, 2)
        vec = red[:, at + 4 * heads : at + 4 * heads + 4].T
    return (
        out.reshape(inputs.shape),
        gin.reshape(inputs.shape),
        jnp.transpose(qkv, (1, 0, 2)),
        o.T,
        up,
        down.T,
        vec[0],
        vec[1],
        vec[2],
        vec[3],
    )


def solution(mesh):
    dp = mesh.shape["dp"]
    in_specs = (
        P("dp", None, None), P("dp"), P(None, None, "mp"), P("mp", None), P(None, "mp"), P("mp", None),
        P(), P(), P(), P(), P("dp", None, None),
    )
    out_specs = (
        P("dp", None, None), P("dp", None, None), P("dp", None, "mp"), P("mp", "dp"), P("dp", "mp"), P("mp", "dp"),
        P("dp"), P("dp"), P("dp"), P("dp"),
    )

    def step(*args):
        return per_device(dp, *args)

    return jax.shard_map(step, mesh=mesh, in_specs=in_specs, out_specs=out_specs, check_vma=False)
```

```python
import math

import jax
import jax.numpy as jnp
from jax import lax
from jax.experimental import pallas as pl
from jax.experimental.pallas import tpu as pltpu
from jax.sharding import PartitionSpec as P

HD = 64
CTX = 384
EPS = 1e-05
BF = jnp.bfloat16
F32 = jnp.float32
MESH = pl.DeviceIdType.MESH
PAIR = 2 * HD
RB = 256
NB = 128


def nn(a, b):
    return lax.dot_general(a, b, (((1,), (0,)), ((), ())), preferred_element_type=F32)


def nt(a, b):
    return lax.dot_general(a, b, (((1,), (1,)), ((), ())), preferred_element_type=F32)


def tn(a, b):
    return lax.dot_general(a, b, (((0,), (0,)), ((), ())), preferred_element_type=F32)


def unit_rows(rows):
    centre = jnp.mean(rows, axis=-1, keepdims=True)
    centred = rows - centre
    inverse = lax.rsqrt(jnp.mean(centred * centred, axis=-1, keepdims=True) + EPS)
    return centred * inverse, inverse


def norm_backward(grad, unit, inverse, gain):
    u = grad * gain
    first = jnp.mean(u, axis=-1, keepdims=True)
    second = jnp.mean(u * unit, axis=-1, keepdims=True)
    return inverse * (u - first - unit * second)


CHUNKS = (('down', 0, 256), ('up', 0, 256), ('down', 256, 256), ('up', 256, 256), ('down', 512, 512), ('up', 512, 512), ('down', 1024, 512), ('up', 1024, 512), ('out', 0, 384), ('q', 0, 384), ('k', 0, 256), ('k', 256, 128), ('v', 0, 128), ('v', 128, 128), ('v', 256, 128), ('vec', 0, 128))
HOPS = ('x', 'x', 'y', 'y', 'x', 'zx', 'x', 'y', 'y', 'x', 'y', 'x', 'y', 'y', 'y', 'x')
ORDER = ((0, 0), (2, 0), (1, 0), (3, 0), (0, 1), (5, 0), (4, 0), (2, 1), (1, 1), (7, 0), (0, 2), (3, 1), (1, 2), (5, 1), (4, 1), (6, 0), (0, 3), (2, 2), (3, 2), (8, 0), (7, 1), (4, 2), (1, 3), (5, 2), (6, 1), (9, 0), (2, 3), (3, 3), (7, 2), (8, 1), (10, 0), (5, 3), (6, 2), (12, 0), (4, 3), (9, 1), (10, 1), (11, 0), (13, 0), (5, 4), (7, 3), (8, 2), (14, 0), (12, 1), (6, 3), (10, 2), (9, 2), (11, 1), (15, 0), (12, 2), (13, 1), (8, 3), (14, 1), (11, 2), (15, 1), (10, 3), (13, 2), (14, 2), (9, 3), (15, 2), (12, 3), (11, 3), (13, 3), (14, 3), (15, 3))
SERVE = (1, 3, 4, 7, 8, 10, 12, 16, 16, 18, 20, 21, 22, 25, 26, 31, 34, 39, 44, 46, 47, 49, 51, 53, 55)


class Plan:
    def __init__(self, tables, seq, width, heads, hidden, dp):
        self.tables, self.seq, self.width, self.heads, self.hidden, self.dp = tables, seq, width, heads, hidden, dp
        self.rows = tables * seq
        self.share = width // dp
        self.fused = dp == 16 and self.share % 16 == 0
        self.step = 256
        self.first = {"down": 0, "up": hidden, "out": 2 * hidden}
        for name, before in (("q", "out"), ("k", "q"), ("v", "k"), ("vec", "v")):
            self.first[name] = self.first[before] + heads
        at = self.first["vec"]
        self.z_columns = 0
        self.z_at = []
        if hidden == 1536 and heads == 384:
            widths = CHUNKS
        else:
            widths = (("down", 0, hidden), ("up", 0, hidden), *((n, 0, heads) for n in ("out", "q", "k", "v")), ("vec", 0, 128))
        chunks = [(name, self.first[name] + off, cw) for name, off, cw in widths]
        chunks = [c + (HOPS[i % len(HOPS)],) for i, c in enumerate(chunks)]
        for _, _, cw, kind in chunks:
            self.z_at.append(self.z_columns)
            self.z_columns += cw if kind[0] == "z" else 0
        self.chunks = chunks
        self.columns = at + 128
        self.finish_parts = (8, 4, 1, 1, 1, 1)
        if self.fused:
            shapes = ((self.share, hidden), (self.share, hidden), (self.share, heads), (3, self.share, heads), (8, self.share))
            self.grad_shapes = tuple((a, F32) for a in shapes)
        else:
            self.grad_shapes = (((width, self.columns), BF),)


def layer_kernel(
    plan,
    counts_ref, x_hbm, wqkv_hbm, wout_hbm, wup_hbm, wdown_hbm, cot_hbm, g1_ref, b1_ref, g2_ref, b2_ref,
    out_hbm, gin_hbm, *rest,
):
    grads_hbm, rest = rest[: len(plan.grad_shapes)], rest[len(plan.grad_shapes) :]
    (
        x, wqkv, wout, wup, wdown, gl,
    nrm, q, k, v, prob, ho, resid, gres, glt, n2t, act, glf, vec, work, low_s,
    xs, xr_a, xr_b,
    g, r1, r2, r3, r4, red, vecs,
    in_sem, out_sem, red_sem, xsend, xrecv, send, recv,
    ) = rest
    T, S, D, H, FF = plan.tables, plan.seq, plan.width, plan.heads, plan.hidden
    R = plan.rows
    pairs = H // PAIR
    dp = lax.axis_index("dp")
    mp = lax.axis_index("mp")
    xx, yy, zz = lax.rem(dp, 2), lax.rem(lax.div(dp, 2), 2), lax.div(dp, 4)
    partner = (dp, 1 - mp)

    def chip(z, y, x_):
        return (z * 4 + y * 2 + x_, mp)

    x_peer, y_peer = chip(zz, yy, 1 - xx), chip(zz, 1 - yy, xx)
    z_peers = [chip(lax.rem(zz + d, 4), yy, xx) for d in (1, 2, 3)]
    peers = [partner] + ([x_peer, y_peer] + z_peers if plan.fused else [])

    loads = [
        pltpu.make_async_copy(a, b, in_sem.at[i])
        for i, (a, b) in enumerate(
            ((x_hbm, x), (wqkv_hbm, wqkv), (wout_hbm, wout), (cot_hbm, gl), (wup_hbm, wup), (wdown_hbm, wdown))
        )
    ]
    for c in loads:
        c.start()
    barrier = pltpu.get_barrier_semaphore()
    for n in peers:
        pl.semaphore_signal(barrier, inc=1, device_id=n, device_id_type=MESH)

    def remote(src, dst, ss, rs, dev):
        return pltpu.make_async_remote_copy(src, dst, ss, rs, device_id=dev, device_id_type=MESH)

    def swap(i, t, src, dst):
        rows = pl.ds(t * S, S)
        return remote(src.at[rows], dst.at[rows], xsend.at[i, t], xrecv.at[i, t], partner)

    zh, zl = lax.div(zz, 2), lax.rem(zz, 2)
    outer = lax.rem(zh + zl + 1, 2)

    def store(i):
        name, c0, cw, _ = plan.chunks[i]
        off = c0 - plan.first[name]
        if name == "vec":
            return pltpu.make_async_copy(vecs.at[0:8], grads_hbm[4], red_sem.at[i])
        at = {"down": 0, "up": 1, "out": 2, "q": 3, "k": 3, "v": 3}[name]
        dst = grads_hbm[at].at["qkv".index(name)] if at == 3 else grads_hbm[at]
        return pltpu.make_async_copy(red.at[:, pl.ds(c0, cw)], dst.at[:, pl.ds(off, cw)], red_sem.at[i])

    def finished(i, total):
        name, c0, cw, _ = plan.chunks[i]
        if name == "vec":
            vecs[...] = total.T
        else:
            red[:, pl.ds(c0, cw)] = total
        store(i).start()

    def add(dst, a, b):
        dst[...] = (a[...].astype(F32) + b[...].astype(F32)).astype(BF)

    def flat(i):
        _, c0, cw, kind = plan.chunks[i]
        cs = pl.ds(c0, cw)
        isx = kind == "x"
        other, mine = (1 - yy, yy) if isx else (1 - xx, xx)
        c1 = remote(
            g.at[:, :, :, 1 - xx, :, cs] if isx else g.at[:, :, 1 - yy, :, :, cs],
            r1.at[:, :, :, :, cs], send.at[i, 0], recv.at[i, 0], x_peer if isx else y_peer,
        )
        c2 = remote(r1.at[:, :, other, :, cs], r2.at[:, :, :, cs], send.at[i, 1], recv.at[i, 1], y_peer if isx else x_peer)
        c3 = []
        for d in (1, 2, 3):
            z = lax.rem(zz + d, 4)
            c3.append(
                remote(r2.at[lax.div(z, 2), lax.rem(z, 2), :, cs], r3.at[d - 1, :, cs], send.at[i, 1 + d], recv.at[i, 1 + d], z_peers[d - 1])
            )

        def add_one():
            c1.wait_recv()

            def part(p):
                def one(j):
                    h, l = lax.div(j, 2), lax.rem(j, 2)
                    own = g.at[h, l, p, xx, :, cs] if isx else g.at[h, l, yy, p, :, cs]
                    add(r1.at[h, l, p, :, cs], own, r1.at[h, l, p, :, cs])

                loop(4, one)

            part(other)
            c2.start()
            part(mine)

        def add_two():
            c2.wait_recv()
            for d in (2, 3, 1, 0):
                z = lax.rem(zz + d, 4)
                h, l = lax.div(z, 2), lax.rem(z, 2)
                add(r2.at[h, l, :, cs], r1.at[h, l, mine, :, cs], r2.at[h, l, :, cs])
                if d:
                    c3[d - 1].start()

        def add_three():
            for c in c3:
                c.wait_recv()
            total = r2[zh, zl, :, cs].astype(F32)
            for d in range(3):
                total = total + r3[d, :, cs].astype(F32)
            finished(i, total)

        def drain():
            for c in (c1, c2, *c3):
                c.wait_send()

        return [c1.start, add_one, add_two, add_three], drain

    def upright(i):
        _, c0, cw, kind = plan.chunks[i]
        cs, zs = pl.ds(c0, cw), pl.ds(plan.z_at[i], cw)
        isx = kind == "zx"
        kept = jnp.where(outer == 1, zh, 1 - zh)
        mate = chip(zh * 2 + 1 - zl, yy, xx)
        across_mid = chip(3 - zz, yy, xx)
        across_end = chip((1 - zh) * 3, yy, xx)
        ca = remote(g.at[1 - kept, :, :, :, :, cs], r1.at[:, :, :, :, cs], send.at[i, 0], recv.at[i, 0], mate)
        end_b = remote(r1.at[1 - zl, :, :, :, cs], r4.at[:, :, :, zs], send.at[i, 1], recv.at[i, 1], mate)
        mid_b = remote(r1.at[1 - zl, :, :, :, cs], r2.at[:, :, :, cs], send.at[i, 1], recv.at[i, 2], across_mid)
        far_b = remote(r1.at[zl, :, :, :, cs], r2.at[:, :, :, cs], send.at[i, 2], recv.at[i, 2], across_end)
        if isx:
            half, single = r2.at[:, 1 - xx, :, cs], r2.at[1 - yy, xx, :, cs]
        else:
            half, single = r2.at[1 - yy, :, :, cs], r2.at[yy, 1 - xx, :, cs]
        cc = remote(half, r3.at[0:2, :, cs], send.at[i, 3], recv.at[i, 3], x_peer if isx else y_peer)
        cd = remote(single, r3.at[2, :, cs], send.at[i, 4], recv.at[i, 4], y_peer if isx else x_peer)

        def add_one():
            ca.wait_recv()

            def one(j):
                l, y, x_ = lax.div(j, 4), lax.rem(lax.div(j, 2), 2), lax.rem(j, 2)
                add(r1.at[l, y, x_, :, cs], g.at[kept, l, y, x_, :, cs], r1.at[l, y, x_, :, cs])

            loop(8, one)

            @pl.when(outer == 1)
            def _():
                end_b.start()

            @pl.when(outer == 0)
            def _():
                mid_b.start()
                far_b.start()

        def add_two():
            mid_b.wait_recv()

            @pl.when(outer == 0)
            def _():
                end_b.wait_recv()

            def part(y, x_):
                @pl.when(outer == 1)
                def _():
                    add(r2.at[y, x_, :, cs], r1.at[zl, y, x_, :, cs], r2.at[y, x_, :, cs])

                @pl.when(outer == 0)
                def _():
                    add(r2.at[y, x_, :, cs], r4.at[y, x_, :, zs], r2.at[y, x_, :, cs])

            for p in range(2):
                part(p, 1 - xx) if isx else part(1 - yy, p)
            cc.start()
            for p in range(2):
                part(p, xx) if isx else part(yy, p)

        def add_three():
            cc.wait_recv()

            def part(p):
                at = r2.at[p, xx, :, cs] if isx else r2.at[yy, p, :, cs]
                add(at, at, r3.at[p, :, cs])

            other, mine = (1 - yy, yy) if isx else (1 - xx, xx)
            part(other)
            cd.start()
            part(mine)

        def add_four():
            cd.wait_recv()
            finished(i, r2[yy, xx, :, cs].astype(F32) + r3[2, :, cs].astype(F32))

        def drain():
            ca.wait_send()

            @pl.when(outer == 1)
            def _():
                end_b.wait_send()

            @pl.when(outer == 0)
            def _():
                mid_b.wait_send()
                far_b.wait_send()

            cc.wait_send()
            cd.wait_send()

        return [ca.start, add_one, add_two, add_three, add_four], drain

    prog = []
    if plan.fused:
        prog = [upright(i) if c[3][0] == "z" else flat(i) for i, c in enumerate(plan.chunks)]

    def due(first, last=None):
        if plan.fused:
            start = SERVE[first - 1] if first else 0
            for i, stage in ORDER[start : SERVE[first] if last is None else len(ORDER)]:
                prog[i][0][stage]()

    def due_in(j, n, first, stride=1):
        for i in range(n):
            if plan.fused and SERVE[first + i * stride] > (SERVE[first + i * stride - 1] if first + i * stride else 0):
                pl.when(j == i)(lambda i=i: due(first + i * stride))

    def loop(n, body):
        def step(i, carry):
            body(i)
            return carry

        lax.fori_loop(0, n, step, 0)

    def put(c0, cw, rows768):
        cs = pl.ds(c0, cw)
        if plan.fused:
            g[:, :, :, :, :, cs] = rows768.astype(BF).reshape(2, 2, 2, 2, plan.share, cw)
        else:
            g[:, cs] = rows768.astype(BF)

    def rows_of(b):
        return pl.ds(pl.multiple_of(b * RB, RB), RB)

    loads[0].wait()
    g1, b1, g2, b2 = (a[...].reshape(1, D) for a in (g1_ref, b1_ref, g2_ref, b2_ref))

    def first_norm(b):
        rs = rows_of(b)
        unit, _ = unit_rows(x[rs, :].astype(F32))
        nrm[rs, :] = (unit * g1 + b1).astype(BF)

    per = S // RB
    for t in range(T):
        for i in range(per):
            first_norm(t * per + i)
        if t == 0:
            loads[1].wait()
        rows, context, kept = slice(t * S, (t + 1) * S), slice(t * S, t * S + CTX), slice(t * CTX, (t + 1) * CTX)
        q[rows, :] = nn(nrm[rows, :], wqkv[0]).astype(BF)
        k[kept, :] = nn(nrm[context, :], wqkv[1]).astype(BF)
        v[kept, :] = nn(nrm[context, :], wqkv[2]).astype(BF)

    n2 = x
    low_p = n2.at[0 : 2 * CTX, 0:S]

    scale = 1.0 / math.sqrt(HD)
    low_lane = lax.broadcasted_iota(jnp.int32, (CTX, PAIR), 1) < HD
    low_row = lax.broadcasted_iota(jnp.int32, (PAIR, CTX), 0) < HD

    def stacked(a):
        zero = jnp.zeros_like(a)
        return jnp.concatenate([jnp.where(low_lane, a, zero), jnp.where(low_lane, zero, a)], axis=0)

    def beside(a):
        at = a.T
        zero = jnp.zeros_like(at)
        return jnp.concatenate([jnp.where(low_row, at, zero), jnp.where(low_row, zero, at)], axis=1)

    def merged(a):
        return jnp.where(low_lane, a[:CTX], a[CTX:])

    def attend_scores(t, h):
        rows, kept, cols = slice(t * S, (t + 1) * S), slice(t * CTX, (t + 1) * CTX), slice(h * PAIR, (h + 1) * PAIR)
        prob[t * pairs + h] = nt(stacked(k[kept, cols]), q[rows, cols])

    def attend(t, h):
        rows, kept, cols = slice(t * S, (t + 1) * S), slice(t * CTX, (t + 1) * CTX), slice(h * PAIR, (h + 1) * PAIR)
        slot = t * pairs + h
        for i in range(2):
            part = slice(i * CTX, (i + 1) * CTX)
            s = prob[slot, part, :]
            e = jnp.exp((s - jnp.max(s, axis=0, keepdims=True)) * scale)
            p = e * (1.0 / jnp.sum(e, axis=0, keepdims=True))
            prob[slot, part, :] = p
            low_s[part, :] = p.astype(BF)
        ho[rows, cols] = nn(beside(v[kept, cols]), low_s[...]).T.astype(BF)

    order = [(t, h) for t in range(T) for h in range(pairs)]
    attend_scores(*order[0])
    for j, (t, h) in enumerate(order):
        if j + 1 < len(order):
            attend_scores(*order[j + 1])
        attend(t, h)
        if h == pairs - 1:
            if t == 0:
                loads[2].wait()
                pl.semaphore_wait(barrier, len(peers))
            rows = slice(t * S, (t + 1) * S)
            xs[rows, :] = nn(ho[rows, :], wout[...]).astype(BF)
            swap(0, t, xs, xr_a).start()

    loads[3].wait()

    def mask(b):
        rs = rows_of(b)
        pos = lax.broadcasted_iota(jnp.int32, (RB, 1), 0) + lax.rem(b * RB, S)
        live = pos < CTX + counts_ref[lax.div(b * RB, S)]
        kept = jnp.where(live, gl[rs, :].astype(F32), 0.0).astype(BF)
        gl[rs, :] = kept
        glt[:, rs] = kept.T

    loop(R // RB, mask)

    def second_norm(b):
        rs = rows_of(b)
        r = x[rs, :].astype(F32) + (xs[rs, :].astype(F32) + xr_a[rs, :].astype(F32))
        resid[rs, :] = r
        unit, _ = unit_rows(r)
        n2[rs, :] = (unit * g2 + b2).astype(BF)

    for t in range(T):
        swap(0, t, xs, xr_a).wait_recv()
        loop(per, lambda i, t=t: second_norm(t * per + i))
    loads[4].wait()
    loads[5].wait()

    step = plan.step
    steps = FF // step

    def hidden_of(c):
        return pl.ds(c * step if isinstance(c, int) else pl.multiple_of(c * step, step), step)

    def lift(c):
        work[0] = nn(n2[...], wup[:, hidden_of(c)])

    def pull(c):
        work[1] = nt(gl[...], wdown[hidden_of(c), :])

    def bend(c):
        cs = hidden_of(c)
        for b in range(R // RB):
            rs = slice(b * RB, (b + 1) * RB)
            lifted = work[0, rs, :]
            half = 0.5 + 0.5 * lax.erf(lifted * (1.0 / math.sqrt(2.0)))
            act[rs, cs] = (lifted * half).astype(BF)
            work[2, rs, :] = half + lifted * (jnp.exp(-0.5 * lifted * lifted) * (1.0 / math.sqrt(2.0 * math.pi)))

    def slope(c):
        cs = hidden_of(c)
        for b in range(R // RB):
            rs = slice(b * RB, (b + 1) * RB)
            glf[rs, cs] = (work[2, rs, :] * work[1, rs, :]).astype(BF)

    def grad(c0, left_t, right, cols, cw):
        put(c0, cw, nn(left_t[...], right[:, cols]))

    def feed(c):
        off = pl.multiple_of(c * step, step)
        lift(c)
        pull(c)
        bend(c)
        grad(plan.first["down"] + off, glt, act, hidden_of(c), step)
        slope(c)
        grad(plan.first["up"] + off, n2t, glf, hidden_of(c), step)
        due_in(c, steps, 0)

    for b in range(R // RB):
        n2t[:, b * RB : (b + 1) * RB] = n2[b * RB : (b + 1) * RB, :].T
    loop(steps, feed)
    point = steps

    for t in range(T):
        swap(0, t, xs, xr_a).wait_send()
    tiles = D // 256
    for t in range(T):
        rows = slice(t * S, (t + 1) * S)

        def body(j, rows=rows):
            cs = pl.ds(pl.multiple_of(j * 256, 256), 256)
            xs[rows, cs] = nt(glf[rows, :], wup[cs, :]).astype(BF)

        loop(tiles, body)
        swap(1, t, xs, xr_b).start()
        due(point)
        point += 1

    vec[...] = jnp.zeros_like(vec)

    def second_back(b):
        rs = pl.ds(pl.multiple_of(b * NB, NB), NB)
        grad_norm = xs[rs, :].astype(F32) + xr_b[rs, :].astype(F32)
        unit, inverse = unit_rows(resid[rs, :])
        vec[2:3, :] += jnp.sum(grad_norm * unit, axis=0, keepdims=True)
        vec[3:4, :] += jnp.sum(grad_norm, axis=0, keepdims=True)
        total = gl[rs, :].astype(F32) + norm_backward(grad_norm, unit, inverse, g2)
        gres[rs, :] = total
        gl[rs, :] = total.astype(BF)

    for t in range(T):
        swap(1, t, xs, xr_b).wait_recv()
        loop(S // NB, lambda i, t=t: second_back(t * (S // NB) + i))
        due(point)
        point += 1

    gh, gq, gk, gv = 0, H, 2 * H, 3 * H
    for t in range(T):
        rows = slice(t * S, (t + 1) * S)
        glf[rows, gh : gh + H] = nt(gl[rows, :], wout[...]).astype(BF)
    put(plan.first["out"], H, tn(gl[...], ho[...]))
    again = pltpu.make_async_copy(x_hbm, gl, in_sem.at[6])
    again.start()
    due(point)
    point += 1

    half = S // 2

    def back_scores(j, i):
        t, h = order[j]
        rows, kept, cols = slice(t * S, (t + 1) * S), slice(t * CTX, (t + 1) * CTX), slice(h * PAIR, (h + 1) * PAIR)
        part = slice(t * S + i * half, t * S + (i + 1) * half)
        work[(2 * j + i) % 3, 0 : 2 * CTX, :] = nt(stacked(v[kept, cols]), glf[part, gh + h * PAIR : gh + (h + 1) * PAIR])

    def attend_back(j):
        t, h = order[j]
        rows, context = slice(t * S, (t + 1) * S), slice(t * S, t * S + CTX)
        kept, cols = slice(t * CTX, (t + 1) * CTX), slice(h * PAIR, (h + 1) * PAIR)
        for i in range(2):
            if j + 1 < len(order):
                back_scores(j + 1, i)
            side = slice(i * half, (i + 1) * half)
            for n in range(2):
                part = slice(n * CTX, (n + 1) * CTX)
                p = prob[j, part, side]
                b = work[(2 * j + i) % 3, part, :]
                low_p[part, side] = p.astype(BF)
                low_s[part, side] = (p * (b - jnp.sum(p * b, axis=0, keepdims=True))).astype(BF)

        def at(first):
            return slice(first + h * PAIR, first + (h + 1) * PAIR)

        glf[rows, at(gq)] = (nn(beside(k[kept, cols]), low_s[...]).T * scale).astype(BF)
        glf[context, at(gk)] = (merged(nn(low_s[...], q[rows, cols])) * scale).astype(BF)
        glf[context, at(gv)] = merged(nn(low_p[...], glf[rows, at(gh)])).astype(BF)

    back_scores(0, 0)
    back_scores(0, 1)
    for j in range(len(order)):
        attend_back(j)
        if j % 2 == 1:
            due(point)
            point += 1

    for b in range(R // RB):
        n2t[:, b * RB : (b + 1) * RB] = nrm[b * RB : (b + 1) * RB, :].T
    grad(plan.first["q"], n2t, glf, slice(gq, gq + H), H)
    due(point)

    def grad_context(name, r0):
        total = None
        for t in range(T):
            part = nn(n2t[:, t * S : t * S + CTX], glf[t * S : t * S + CTX, r0 : r0 + H])
            total = part if total is None else total + part
        put(plan.first[name], H, total)

    grad_context("k", gk)
    grad_context("v", gv)
    due(point + 1)
    point += 2

    for t in range(T):
        swap(1, t, xs, xr_b).wait_send()
    for t in range(T):
        rows = slice(t * S, (t + 1) * S)
        ctx = slice(t * S, t * S + CTX)

        def body(j, t=t, rows=rows, ctx=ctx):
            cs = pl.ds(pl.multiple_of(j * 256, 256), 256)
            part = nt(glf[rows, gq : gq + H], wqkv[0, cs, :])
            extra = nt(glf[ctx, gk : gk + H], wqkv[1, cs, :]) + nt(glf[ctx, gv : gv + H], wqkv[2, cs, :])
            xs[ctx, cs] = (part[:CTX] + extra).astype(BF)
            xs[t * S + CTX : (t + 1) * S, cs] = part[CTX:].astype(BF)

        loop(tiles, body)
        swap(3, t, xs, xr_a).start()
        due(point)
        point += 1

    def feed_out(t, point):
        rows = slice(t * S, (t + 1) * S)

        def body(j):
            cs = pl.ds(pl.multiple_of(j * 256, 256), 256)
            nrm[rows, cs] = nn(act[rows, :], wdown[:, cs]).astype(BF)

        loop(tiles, body)
        due(point)

    feed_out(0, point)
    point += 1

    def first_back(b):
        rs = pl.ds(pl.multiple_of(b * NB, NB), NB)
        grad_norm = xs[rs, :].astype(F32) + xr_a[rs, :].astype(F32)
        unit, inverse = unit_rows(gl[rs, :].astype(F32))
        vec[0:1, :] += jnp.sum(grad_norm * unit, axis=0, keepdims=True)
        vec[1:2, :] += jnp.sum(grad_norm, axis=0, keepdims=True)
        gres[rs, :] = gres[rs, :] + norm_backward(grad_norm, unit, inverse, g1)

    again.wait()
    for t in range(T):
        swap(3, t, xs, xr_a).wait_recv()
        loop(S // NB, lambda i, t=t: first_back(t * (S // NB) + i))
        due(point)
        point += 1
    swap(2, 0, nrm, xr_b).start()
    store_gin = pltpu.make_async_copy(gres, gin_hbm, out_sem.at[1])
    store_gin.start()
    put(plan.first["vec"], 128, jnp.concatenate([vec[...], jnp.zeros((128 - vec.shape[0], D), F32)], axis=0).T)
    due(point)
    point += 1

    for t in range(1, T):
        feed_out(t, point)
        point += 1
        swap(2, t, nrm, xr_b).start()

    def output(b):
        rs = rows_of(b)
        pos = lax.broadcasted_iota(jnp.int32, (RB, 1), 0) + lax.rem(b * RB, S)
        live = pos < CTX + counts_ref[lax.div(b * RB, S)]
        total = resid[rs, :] + (nrm[rs, :].astype(F32) + xr_b[rs, :].astype(F32))
        n2[rs, :] = jnp.where(live, total, 0.0).astype(BF)

    for t in range(T):
        swap(2, t, nrm, xr_b).wait_recv()
        loop(per, lambda i, t=t: output(t * per + i))
        due(point)
        point += 1
    store_out = pltpu.make_async_copy(n2, out_hbm, out_sem.at[0])
    store_out.start()
    assert point == len(SERVE)
    due(point, True)

    if not plan.fused:
        store = lambda i: pltpu.make_async_copy(g, grads_hbm[0], red_sem.at[0])
        store(0).start()
    for p in prog:
        p[1]()
    for t in range(T):
        swap(2, t, nrm, xr_b).wait_send()
        swap(3, t, xs, xr_a).wait_send()
    store_out.wait()
    store_gin.wait()
    for i in range(max(1, len(prog))):
        store(i).wait()


def run_layer(plan, counts, x, wqkv, wout, wup, wdown, cot, gains):
    R, D, H, FF, W = plan.rows, plan.width, plan.heads, plan.hidden, plan.columns
    V = pltpu.VMEM
    DMA = pltpu.SemaphoreType.DMA
    n = len(plan.chunks)
    share = plan.share
    if plan.fused:
        gshape = (2, 2, 2, 2, share, W)
        comm = [V((2, 2, 2, share, W), BF), V((2, 2, share, W), BF), V((3, share, W), BF)]
        comm += [V((2, 2, share, plan.z_columns), BF), V((share, W), F32), V((128, share), F32)]
    else:
        gshape = (D, W)
        comm = [V((8, 128), F32)] * 6
    scratch = [
        V((R, D), BF), V((3, D, H), BF), V((H, D), BF), V((D, FF), BF), V((FF, D), BF), V((R, D), BF),
        V((R, D), BF), V((R, H), BF), V((plan.tables * CTX, H), BF), V((plan.tables * CTX, H), BF),
        V((plan.tables * (H // PAIR), 2 * CTX, plan.seq), F32), V((R, H), BF), V((R, D), F32), V((R, D), F32),
        V((D, R), BF), V((D, R), BF), V((R, FF), BF), V((R, FF), BF), V((8, D), F32), V((3, R, 256), F32), V((2 * CTX, plan.seq), BF),
        V((R, D), BF), V((R, D), BF), V((R, D), BF),
        V(gshape, BF), *comm,
        DMA((7,)), DMA((2,)), DMA((n,)), DMA((4, plan.tables)), DMA((4, plan.tables)),
        DMA((n, 5)), DMA((n, 5)),
    ]
    hbm = pl.BlockSpec(memory_space=pl.ANY)

    def kernel(*refs):
        layer_kernel(plan, *refs)

    return pl.pallas_call(
        kernel,
        out_shape=(
            jax.ShapeDtypeStruct((R, D), BF),
            jax.ShapeDtypeStruct((R, D), F32),
            *(jax.ShapeDtypeStruct(*a) for a in plan.grad_shapes),
        ),
        in_specs=[pl.BlockSpec(memory_space=pltpu.SMEM)] + [hbm] * 6 + [pl.BlockSpec(memory_space=pltpu.VMEM)] * 4,
        out_specs=(hbm,) * (2 + len(plan.grad_shapes)),
        scratch_shapes=scratch,
        compiler_params=pltpu.CompilerParams(collective_id=0, has_side_effects=True, vmem_limit_bytes=67043328),
        name="layer",
    )(counts, x, wqkv, wout, wup, wdown, cot, *gains)


def finish_kernel(plan, *refs):
    n = 6
    src, vec_ref, dst, vec_out = refs[:n], refs[n], refs[n + 1 : 2 * n + 1], refs[2 * n + 1 : 2 * n + 5]
    bufs, in_sem, out_sem = refs[2 * n + 5 : 3 * n + 5], refs[3 * n + 5], refs[3 * n + 6]
    moves = []
    for i in range(n):
        rows = src[i].shape[0]
        parts = plan.finish_parts[i]
        for j in range(parts):
            moves.append((i, pl.ds(j * (rows // parts), rows // parts)))
    loads, stores = [], []
    for m, (i, rows) in enumerate(moves):
        loads.append(pltpu.make_async_copy(src[i].at[rows], bufs[i].at[rows], in_sem.at[m]))
        stores.append(pltpu.make_async_copy(bufs[i].at[rows], dst[i].at[rows], out_sem.at[m]))
    for c in loads:
        c.start()
    for i in range(4):
        vec_out[i][...] = vec_ref[i, :]
    for a, b in zip(loads, stores):
        a.wait()
        b.start()
    for c in stores:
        c.wait()


def finish(plan, shape, out, gin, down, up, o, qkv, vec):
    arrays = (gin, out, up, down, qkv, o)
    n = sum(plan.finish_parts)
    hbm = pl.BlockSpec(memory_space=pltpu.HBM)
    vmem = pl.BlockSpec(memory_space=pltpu.VMEM)
    share = plan.share

    def kernel(*refs):
        finish_kernel(plan, *refs)

    gin, out, up, down, qkv, o, *norms = pl.pallas_call(
        kernel,
        out_shape=tuple(jax.ShapeDtypeStruct(a.shape, a.dtype) for a in arrays)
        + tuple(jax.ShapeDtypeStruct((share,), F32) for _ in range(4)),
        in_specs=[hbm] * 6 + [vmem],
        out_specs=(hbm,) * 6 + (vmem,) * 4,
        scratch_shapes=[pltpu.VMEM(a.shape, a.dtype) for a in arrays]
        + [pltpu.SemaphoreType.DMA((n,)), pltpu.SemaphoreType.DMA((n,))],
        name="finish",
    )(*arrays, vec)
    return (out.reshape(shape), gin.reshape(shape), jnp.transpose(qkv, (1, 0, 2)), o.T, up, down.T, *norms)


def per_device(dp, inputs, counts, w_qkv, w_out, w_up, w_down, gain_one, shift_one, gain_two, shift_two, cotangent):
    tables, seq, width = inputs.shape
    heads, hidden = w_out.shape[0], w_up.shape[1]
    plan = Plan(tables, seq, width, heads, hidden, dp)
    rows = tables * seq
    gains = (gain_one, shift_one, gain_two, shift_two)
    out, gin, *grads = run_layer(
        plan,
        counts,
        inputs.reshape(rows, width),
        jnp.transpose(w_qkv, (1, 0, 2)),
        w_out,
        w_up,
        w_down,
        cotangent.reshape(rows, width),
        gains,
    )
    if plan.fused:
        down, up, o, qkv, vec = grads
        return finish(plan, inputs.shape, out, gin, down, up, o, qkv, vec)
    else:
        red = lax.psum_scatter(grads[0].astype(F32), "dp", scatter_dimension=0, tiled=True)
        at = 2 * hidden
        down, up, o = red[:, :hidden], red[:, hidden:at], red[:, at : at + heads]
        qkv = red[:, at + heads : at + 4 * heads].reshape(-1, 3, heads).transpose(1, 0, 2)
        vec = red[:, at + 4 * heads : at + 4 * heads + 4].T
    return (
        out.reshape(inputs.shape),
        gin.reshape(inputs.shape),
        jnp.transpose(qkv, (1, 0, 2)),
        o.T,
        up,
        down.T,
        vec[0],
        vec[1],
        vec[2],
        vec[3],
    )


def solution(mesh):
    dp = mesh.shape["dp"]
    in_specs = (
        P("dp", None, None), P("dp"), P(None, None, "mp"), P("mp", None), P(None, "mp"), P("mp", None),
        P(), P(), P(), P(), P("dp", None, None),
    )
    out_specs = (
        P("dp", None, None), P("dp", None, None), P("dp", None, "mp"), P("mp", "dp"), P("dp", "mp"), P("mp", "dp"),
        P("dp"), P("dp"), P("dp"), P("dp"),
    )

    def step(*args):
        return per_device(dp, *args)

    return jax.shard_map(step, mesh=mesh, in_specs=in_specs, out_specs=out_specs, check_vma=False)
```

```python
import math

import jax
import jax.numpy as jnp
from jax import lax
from jax.experimental import pallas as pl
from jax.experimental.pallas import tpu as pltpu
from jax.sharding import PartitionSpec as P

HD = 64
CTX = 384
EPS = 1e-05
BF = jnp.bfloat16
F32 = jnp.float32
MESH = pl.DeviceIdType.MESH
PAIR = 2 * HD
RB = 256
NB = 128


def nn(a, b):
    return lax.dot_general(a, b, (((1,), (0,)), ((), ())), preferred_element_type=F32)


def nt(a, b):
    return lax.dot_general(a, b, (((1,), (1,)), ((), ())), preferred_element_type=F32)


def tn(a, b):
    return lax.dot_general(a, b, (((0,), (0,)), ((), ())), preferred_element_type=F32)


def unit_rows(rows):
    centre = jnp.mean(rows, axis=-1, keepdims=True)
    centred = rows - centre
    inverse = lax.rsqrt(jnp.mean(centred * centred, axis=-1, keepdims=True) + EPS)
    return centred * inverse, inverse


def norm_backward(grad, unit, inverse, gain):
    u = grad * gain
    first = jnp.mean(u, axis=-1, keepdims=True)
    second = jnp.mean(u * unit, axis=-1, keepdims=True)
    return inverse * (u - first - unit * second)


CHUNKS = (('down', 0, 256), ('up', 0, 256), ('down', 256, 256), ('up', 256, 256), ('down', 512, 512), ('up', 512, 512), ('down', 1024, 512), ('up', 1024, 512), ('out', 0, 384), ('q', 0, 128), ('q', 128, 256), ('k', 0, 256), ('k', 256, 128), ('v', 0, 128), ('v', 128, 128), ('v', 256, 128))
HOPS = ('y', 'x', 'y', 'zy', 'x', 'zx', 'x', 'y', 'y', 'zx', 'x', 'x', 'y', 'y', 'y', 'y')
ORDER = ((0, 0), (1, 0), (3, 0), (2, 0), (0, 1), (1, 1), (5, 0), (4, 0), (3, 1), (0, 2), (1, 2), (2, 1), (7, 0), (5, 1), (6, 0), (3, 2), (4, 1), (2, 2), (7, 1), (8, 0), (3, 3), (4, 2), (5, 2), (0, 3), (1, 3), (6, 1), (2, 3), (7, 2), (10, 0), (3, 4), (8, 1), (12, 0), (9, 0), (5, 3), (13, 0), (4, 3), (6, 2), (11, 0), (14, 0), (10, 1), (12, 1), (5, 4), (7, 3), (9, 1), (8, 2), (13, 1), (15, 0), (6, 3), (14, 1), (11, 1), (9, 2), (10, 2), (12, 2), (13, 2), (14, 2), (15, 1), (9, 3), (8, 3), (11, 2), (10, 3), (15, 2), (9, 4), (12, 3), (13, 3), (14, 3), (11, 3), (15, 3))
SERVE = (2, 4, 4, 8, 9, 13, 13, 15, 17, 18, 20, 21, 23, 26, 29, 34, 35, 39, 41, 44, 47, 47, 49, 52, 53, 56, 59, 59, 61, 62, 65, 65, 65)


class Plan:
    def __init__(self, tables, seq, width, heads, hidden, dp):
        self.tables, self.seq, self.width, self.heads, self.hidden, self.dp = tables, seq, width, heads, hidden, dp
        self.rows = tables * seq
        self.share = width // dp
        self.fused = dp == 16 and self.share % 16 == 0
        self.step = 256
        self.first = {"down": 0, "up": hidden, "out": 2 * hidden}
        for name, before in (("q", "out"), ("k", "q"), ("v", "k"), ("vec", "v")):
            self.first[name] = self.first[before] + heads
        at = self.first["vec"]
        self.z_columns = 0
        self.z_at = []
        if hidden == 1536 and heads == 384:
            widths = CHUNKS
        else:
            widths = (("down", 0, hidden), ("up", 0, hidden), *((n, 0, heads) for n in ("out", "q", "k", "v")))
        chunks = [(name, self.first[name] + off, cw) for name, off, cw in widths]
        chunks = [c + (HOPS[i % len(HOPS)],) for i, c in enumerate(chunks)]
        for _, _, cw, kind in chunks:
            self.z_at.append(self.z_columns)
            self.z_columns += cw if kind[0] == "z" else 0
        self.chunks = chunks
        self.columns = at if self.fused else at + 128
        self.finish_parts = (2, 1, 1, 1, 1, 1)
        if self.fused:
            shapes = ((self.share, hidden), (self.share, hidden), (self.share, heads), (3, self.share, heads), (8, 128))
            self.grad_shapes = tuple((a, F32) for a in shapes)
        else:
            self.grad_shapes = (((width, self.columns), BF),)


def layer_kernel(
    plan,
    counts_ref, x_hbm, wqkv_hbm, wout_hbm, wup_hbm, wdown_hbm, cot_hbm, g1_ref, b1_ref, g2_ref, b2_ref,
    out_hbm, gin_hbm, *rest,
):
    grads_hbm, rest = rest[: len(plan.grad_shapes)], rest[len(plan.grad_shapes) :]
    (
        x, wqkv, wout, wup, wdown, gl,
    nrm, q, k, v, prob, ho, resid, gres, glt, n2t, act, glf, vec, work, low_s,
    xs, xr_a, xr_b,
    g, r1, r2, r3, r4, red, vmine, vtheirs,
    in_sem, out_sem, red_sem, xsend, xrecv, send, recv, vsend, vrecv,
    ) = rest
    T, S, D, H, FF = plan.tables, plan.seq, plan.width, plan.heads, plan.hidden
    R = plan.rows
    pairs = H // PAIR
    dp = lax.axis_index("dp")
    mp = lax.axis_index("mp")
    xx, yy, zz = lax.rem(dp, 2), lax.rem(lax.div(dp, 2), 2), lax.div(dp, 4)
    partner = (dp, 1 - mp)

    def chip(z, y, x_):
        return (z * 4 + y * 2 + x_, mp)

    x_peer, y_peer = chip(zz, yy, 1 - xx), chip(zz, 1 - yy, xx)
    z_peers = [chip(lax.rem(zz + d, 4), yy, xx) for d in (1, 2, 3)]
    others = [(lax.rem(dp + d, plan.dp), mp) for d in range(1, plan.dp)] if plan.fused else []
    peers = [partner] + others

    loads = [
        pltpu.make_async_copy(a, b, in_sem.at[i])
        for i, (a, b) in enumerate(
            ((x_hbm, x), (wqkv_hbm, wqkv), (wout_hbm, wout), (cot_hbm, gl), (wup_hbm, wup), (wdown_hbm, wdown))
        )
    ]
    for c in loads[:2]:
        c.start()
    barrier = pltpu.get_barrier_semaphore()
    for n in peers:
        pl.semaphore_signal(barrier, inc=1, device_id=n, device_id_type=MESH)

    def remote(src, dst, ss, rs, dev):
        return pltpu.make_async_remote_copy(src, dst, ss, rs, device_id=dev, device_id_type=MESH)

    def swap(i, t, src, dst):
        rows = pl.ds(t * S, S)
        return remote(src.at[rows], dst.at[rows], xsend.at[i, t], xrecv.at[i, t], partner)

    zh, zl = lax.div(zz, 2), lax.rem(zz, 2)
    outer = lax.rem(zh + zl + 1, 2)

    def store(i):
        name, c0, cw, _ = plan.chunks[i]
        off = c0 - plan.first[name]
        at = {"down": 0, "up": 1, "out": 2, "q": 3, "k": 3, "v": 3}[name]
        dst = grads_hbm[at].at["qkv".index(name)] if at == 3 else grads_hbm[at]
        return pltpu.make_async_copy(red.at[:, pl.ds(c0, cw)], dst.at[:, pl.ds(off, cw)], red_sem.at[i])

    def finished(i, total):
        _, c0, cw, _ = plan.chunks[i]
        red[:, pl.ds(c0, cw)] = total
        store(i).start()

    def add(dst, a, b):
        dst[...] = (a[...].astype(F32) + b[...].astype(F32)).astype(BF)

    def flat(i):
        _, c0, cw, kind = plan.chunks[i]
        cs = pl.ds(c0, cw)
        isx = kind == "x"
        other, mine = (1 - yy, yy) if isx else (1 - xx, xx)
        c1 = remote(
            g.at[:, :, :, 1 - xx, :, cs] if isx else g.at[:, :, 1 - yy, :, :, cs],
            r1.at[:, :, :, :, cs], send.at[i, 0], recv.at[i, 0], x_peer if isx else y_peer,
        )
        c2 = remote(r1.at[:, :, other, :, cs], r2.at[:, :, :, cs], send.at[i, 1], recv.at[i, 1], y_peer if isx else x_peer)
        c3 = []
        for d in (1, 2, 3):
            z = lax.rem(zz + d, 4)
            c3.append(
                remote(r2.at[lax.div(z, 2), lax.rem(z, 2), :, cs], r3.at[d - 1, :, cs], send.at[i, 1 + d], recv.at[i, 1 + d], z_peers[d - 1])
            )

        def add_one():
            c1.wait_recv()

            def part(p):
                def one(j):
                    h, l = lax.div(j, 2), lax.rem(j, 2)
                    own = g.at[h, l, p, xx, :, cs] if isx else g.at[h, l, yy, p, :, cs]
                    add(r1.at[h, l, p, :, cs], own, r1.at[h, l, p, :, cs])

                loop(4, one)

            part(other)
            c2.start()
            part(mine)

        def add_two():
            c2.wait_recv()
            for d in (2, 3, 1, 0):
                z = lax.rem(zz + d, 4)
                h, l = lax.div(z, 2), lax.rem(z, 2)
                add(r2.at[h, l, :, cs], r1.at[h, l, mine, :, cs], r2.at[h, l, :, cs])
                if d:
                    c3[d - 1].start()

        def add_three():
            for c in c3:
                c.wait_recv()
            total = r2[zh, zl, :, cs].astype(F32)
            for d in range(3):
                total = total + r3[d, :, cs].astype(F32)
            finished(i, total)

        def drain():
            for c in (c1, c2, *c3):
                c.wait_send()

        return [c1.start, add_one, add_two, add_three], drain

    def upright(i):
        _, c0, cw, kind = plan.chunks[i]
        cs, zs = pl.ds(c0, cw), pl.ds(plan.z_at[i], cw)
        isx = kind == "zx"
        kept = jnp.where(outer == 1, zh, 1 - zh)
        mate = chip(zh * 2 + 1 - zl, yy, xx)
        across_mid = chip(3 - zz, yy, xx)
        across_end = chip((1 - zh) * 3, yy, xx)
        ca = remote(g.at[1 - kept, :, :, :, :, cs], r1.at[:, :, :, :, cs], send.at[i, 0], recv.at[i, 0], mate)
        end_b = remote(r1.at[1 - zl, :, :, :, cs], r4.at[:, :, :, zs], send.at[i, 1], recv.at[i, 1], mate)
        mid_b = remote(r1.at[1 - zl, :, :, :, cs], r2.at[:, :, :, cs], send.at[i, 1], recv.at[i, 2], across_mid)
        far_b = remote(r1.at[zl, :, :, :, cs], r2.at[:, :, :, cs], send.at[i, 2], recv.at[i, 2], across_end)
        if isx:
            half, single = r2.at[:, 1 - xx, :, cs], r2.at[1 - yy, xx, :, cs]
        else:
            half, single = r2.at[1 - yy, :, :, cs], r2.at[yy, 1 - xx, :, cs]
        cc = remote(half, r3.at[0:2, :, cs], send.at[i, 3], recv.at[i, 3], x_peer if isx else y_peer)
        cd = remote(single, r3.at[2, :, cs], send.at[i, 4], recv.at[i, 4], y_peer if isx else x_peer)

        def add_one():
            ca.wait_recv()

            def one(j):
                l, y, x_ = lax.div(j, 4), lax.rem(lax.div(j, 2), 2), lax.rem(j, 2)
                add(r1.at[l, y, x_, :, cs], g.at[kept, l, y, x_, :, cs], r1.at[l, y, x_, :, cs])

            loop(8, one)

            @pl.when(outer == 1)
            def _():
                end_b.start()

            @pl.when(outer == 0)
            def _():
                mid_b.start()
                far_b.start()

        def add_two():
            mid_b.wait_recv()

            @pl.when(outer == 0)
            def _():
                end_b.wait_recv()

            def part(y, x_):
                @pl.when(outer == 1)
                def _():
                    add(r2.at[y, x_, :, cs], r1.at[zl, y, x_, :, cs], r2.at[y, x_, :, cs])

                @pl.when(outer == 0)
                def _():
                    add(r2.at[y, x_, :, cs], r4.at[y, x_, :, zs], r2.at[y, x_, :, cs])

            for p in range(2):
                part(p, 1 - xx) if isx else part(1 - yy, p)
            cc.start()
            for p in range(2):
                part(p, xx) if isx else part(yy, p)

        def add_three():
            cc.wait_recv()

            def part(p):
                at = r2.at[p, xx, :, cs] if isx else r2.at[yy, p, :, cs]
                add(at, at, r3.at[p, :, cs])

            other, mine = (1 - yy, yy) if isx else (1 - xx, xx)
            part(other)
            cd.start()
            part(mine)

        def add_four():
            cd.wait_recv()
            finished(i, r2[yy, xx, :, cs].astype(F32) + r3[2, :, cs].astype(F32))

        def drain():
            ca.wait_send()

            @pl.when(outer == 1)
            def _():
                end_b.wait_send()

            @pl.when(outer == 0)
            def _():
                mid_b.wait_send()
                far_b.wait_send()

            cc.wait_send()
            cd.wait_send()

        return [ca.start, add_one, add_two, add_three, add_four], drain

    prog = []
    if plan.fused:
        prog = [upright(i) if c[3][0] == "z" else flat(i) for i, c in enumerate(plan.chunks)]

    def due(first, last=None):
        if plan.fused:
            start = SERVE[first - 1] if first else 0
            for i, stage in ORDER[start : SERVE[first] if last is None else len(ORDER)]:
                prog[i][0][stage]()

    def due_in(j, n, first, stride=1):
        for i in range(n):
            if plan.fused and SERVE[first + i * stride] > (SERVE[first + i * stride - 1] if first + i * stride else 0):
                pl.when(j == i)(lambda i=i: due(first + i * stride))

    def loop(n, body):
        def step(i, carry):
            body(i)
            return carry

        lax.fori_loop(0, n, step, 0)

    def put(c0, cw, rows768):
        cs = pl.ds(c0, cw)
        if plan.fused:
            g[:, :, :, :, :, cs] = rows768.astype(BF).reshape(2, 2, 2, 2, plan.share, cw)
        else:
            g[:, cs] = rows768.astype(BF)

    def rows_of(b):
        return pl.ds(pl.multiple_of(b * RB, RB), RB)

    loads[0].wait()
    for c in loads[2:]:
        c.start()
    g1, b1, g2, b2 = (a[...].reshape(1, D) for a in (g1_ref, b1_ref, g2_ref, b2_ref))

    def first_norm(b):
        rs = rows_of(b)
        unit, _ = unit_rows(x[rs, :].astype(F32))
        nrm[rs, :] = (unit * g1 + b1).astype(BF)

    per = S // RB
    for t in range(T):
        for i in range(per):
            first_norm(t * per + i)
        if t == 0:
            loads[1].wait()
        rows, context, kept = slice(t * S, (t + 1) * S), slice(t * S, t * S + CTX), slice(t * CTX, (t + 1) * CTX)
        q[rows, :] = nn(nrm[rows, :], wqkv[0]).astype(BF)
        k[kept, :] = nn(nrm[context, :], wqkv[1]).astype(BF)
        v[kept, :] = nn(nrm[context, :], wqkv[2]).astype(BF)

    n2 = x
    low_p = n2.at[0 : 2 * CTX, 0:S]

    scale = 1.0 / math.sqrt(HD)
    low_lane = lax.broadcasted_iota(jnp.int32, (CTX, PAIR), 1) < HD
    low_row = lax.broadcasted_iota(jnp.int32, (PAIR, CTX), 0) < HD

    def stacked(a):
        zero = jnp.zeros_like(a)
        return jnp.concatenate([jnp.where(low_lane, a, zero), jnp.where(low_lane, zero, a)], axis=0)

    def beside(a):
        at = a.T
        zero = jnp.zeros_like(at)
        return jnp.concatenate([jnp.where(low_row, at, zero), jnp.where(low_row, zero, at)], axis=1)

    def merged(a):
        return jnp.where(low_lane, a[:CTX], a[CTX:])

    def attend_scores(t, h):
        rows, kept, cols = slice(t * S, (t + 1) * S), slice(t * CTX, (t + 1) * CTX), slice(h * PAIR, (h + 1) * PAIR)
        prob[t * pairs + h] = nt(stacked(k[kept, cols]), q[rows, cols])

    def attend(t, h):
        rows, kept, cols = slice(t * S, (t + 1) * S), slice(t * CTX, (t + 1) * CTX), slice(h * PAIR, (h + 1) * PAIR)
        slot = t * pairs + h
        for i in range(2):
            part = slice(i * CTX, (i + 1) * CTX)
            s = prob[slot, part, :]
            e = jnp.exp2((s - jnp.max(s, axis=0, keepdims=True)) * (scale * math.log2(math.e)))
            p = e * (1.0 / jnp.sum(e, axis=0, keepdims=True))
            prob[slot, part, :] = p
            low_s[part, :] = p.astype(BF)
        ho[rows, cols] = nn(beside(v[kept, cols]), low_s[...]).T.astype(BF)

    order = [(t, h) for t in range(T) for h in range(pairs)]
    attend_scores(*order[0])
    for j, (t, h) in enumerate(order):
        if j + 1 < len(order):
            attend_scores(*order[j + 1])
        attend(t, h)
        if h == pairs - 1:
            if t == 0:
                loads[2].wait()
                pl.semaphore_wait(barrier, len(peers))
            rows = slice(t * S, (t + 1) * S)
            xs[rows, :] = nn(ho[rows, :], wout[...]).astype(BF)
            swap(0, t, xs, xr_a).start()

    loads[3].wait()

    def mask(b):
        rs = rows_of(b)
        pos = lax.broadcasted_iota(jnp.int32, (RB, 1), 0) + lax.rem(b * RB, S)
        live = pos < CTX + counts_ref[lax.div(b * RB, S)]
        kept = jnp.where(live, gl[rs, :].astype(F32), 0.0).astype(BF)
        gl[rs, :] = kept
        glt[:, rs] = kept.T

    loop(R // RB, mask)

    def second_norm(b):
        rs = rows_of(b)
        r = x[rs, :].astype(F32) + (xs[rs, :].astype(F32) + xr_a[rs, :].astype(F32))
        resid[rs, :] = r
        unit, _ = unit_rows(r)
        n2[rs, :] = (unit * g2 + b2).astype(BF)

    for t in range(T):
        swap(0, t, xs, xr_a).wait_recv()
        loop(per, lambda i, t=t: second_norm(t * per + i))
    loads[4].wait()
    loads[5].wait()

    step = plan.step
    steps = FF // step

    def hidden_of(c):
        return pl.ds(c * step if isinstance(c, int) else pl.multiple_of(c * step, step), step)

    def lift(c):
        work[0] = nn(n2[...], wup[:, hidden_of(c)])

    def pull(c):
        work[1] = nt(gl[...], wdown[hidden_of(c), :])

    def bend(c):
        cs = hidden_of(c)
        for b in range(R // RB):
            rs = slice(b * RB, (b + 1) * RB)
            lifted = work[0, rs, :]
            half = 0.5 + 0.5 * lax.erf(lifted * (1.0 / math.sqrt(2.0)))
            act[rs, cs] = (lifted * half).astype(BF)
            work[2, rs, :] = half + lifted * (jnp.exp(-0.5 * lifted * lifted) * (1.0 / math.sqrt(2.0 * math.pi)))

    def slope(c):
        cs = hidden_of(c)
        for b in range(R // RB):
            rs = slice(b * RB, (b + 1) * RB)
            glf[rs, cs] = (work[2, rs, :] * work[1, rs, :]).astype(BF)

    def grad(c0, left_t, right, cols, cw):
        put(c0, cw, nn(left_t[...], right[:, cols]))

    def feed(c):
        off = pl.multiple_of(c * step, step)
        lift(c)
        pull(c)
        bend(c)
        grad(plan.first["down"] + off, glt, act, hidden_of(c), step)
        slope(c)
        grad(plan.first["up"] + off, n2t, glf, hidden_of(c), step)
        due_in(c, steps, 0)

    for b in range(R // RB):
        n2t[:, b * RB : (b + 1) * RB] = n2[b * RB : (b + 1) * RB, :].T
    loop(steps, feed)
    point = steps

    for t in range(T):
        swap(0, t, xs, xr_a).wait_send()
    tiles = D // 256
    for t in range(T):
        rows = slice(t * S, (t + 1) * S)

        def body(j, rows=rows):
            cs = pl.ds(pl.multiple_of(j * 256, 256), 256)
            xs[rows, cs] = nt(glf[rows, :], wup[cs, :]).astype(BF)

        loop(tiles, body)
        swap(1, t, xs, xr_b).start()
        due(point)
        point += 1

    vec[...] = jnp.zeros_like(vec)

    def second_back(b):
        rs = pl.ds(pl.multiple_of(b * NB, NB), NB)
        grad_norm = xs[rs, :].astype(F32) + xr_b[rs, :].astype(F32)
        unit, inverse = unit_rows(resid[rs, :])
        vec[2:3, :] += jnp.sum(grad_norm * unit, axis=0, keepdims=True)
        vec[3:4, :] += jnp.sum(grad_norm, axis=0, keepdims=True)
        total = gl[rs, :].astype(F32) + norm_backward(grad_norm, unit, inverse, g2)
        gres[rs, :] = total
        gl[rs, :] = total.astype(BF)

    for t in range(T):
        swap(1, t, xs, xr_b).wait_recv()
        loop(S // NB, lambda i, t=t: second_back(t * (S // NB) + i))
        due(point)
        point += 1

    gh, gq, gk, gv = 0, H, 2 * H, 3 * H
    for t in range(T):
        rows = slice(t * S, (t + 1) * S)
        glf[rows, gh : gh + H] = nt(gl[rows, :], wout[...]).astype(BF)
    put(plan.first["out"], H, tn(gl[...], ho[...]))
    again = pltpu.make_async_copy(x_hbm, gl, in_sem.at[6])
    again.start()
    due(point)
    point += 1

    half = S // 2

    def back_scores(j, i):
        t, h = order[j]
        rows, kept, cols = slice(t * S, (t + 1) * S), slice(t * CTX, (t + 1) * CTX), slice(h * PAIR, (h + 1) * PAIR)
        part = slice(t * S + i * half, t * S + (i + 1) * half)
        work[(2 * j + i) % 3, 0 : 2 * CTX, :] = nt(stacked(v[kept, cols]), glf[part, gh + h * PAIR : gh + (h + 1) * PAIR])

    def attend_back(j):
        t, h = order[j]
        rows, context = slice(t * S, (t + 1) * S), slice(t * S, t * S + CTX)
        kept, cols = slice(t * CTX, (t + 1) * CTX), slice(h * PAIR, (h + 1) * PAIR)
        for i in range(2):
            if j + 1 < len(order):
                back_scores(j + 1, i)
            side = slice(i * half, (i + 1) * half)
            for n in range(2):
                part = slice(n * CTX, (n + 1) * CTX)
                p = prob[j, part, side]
                b = work[(2 * j + i) % 3, part, :]
                low_p[part, side] = p.astype(BF)
                low_s[part, side] = (p * (b - jnp.sum(p * b, axis=0, keepdims=True))).astype(BF)

        def at(first):
            return slice(first + h * PAIR, first + (h + 1) * PAIR)

        glf[rows, at(gq)] = (nn(beside(k[kept, cols]), low_s[...]).T * scale).astype(BF)
        glf[context, at(gk)] = (merged(nn(low_s[...], q[rows, cols])) * scale).astype(BF)
        glf[context, at(gv)] = merged(nn(low_p[...], glf[rows, at(gh)])).astype(BF)

    back_scores(0, 0)
    back_scores(0, 1)
    for j in range(len(order)):
        attend_back(j)
        if j % 2 == 1:
            due(point)
            point += 1

    for b in range(R // RB):
        n2t[:, b * RB : (b + 1) * RB] = nrm[b * RB : (b + 1) * RB, :].T
    grad(plan.first["q"], n2t, glf, slice(gq, gq + H), H)
    due(point)

    def grad_context(name, r0):
        total = None
        for t in range(T):
            part = nn(n2t[:, t * S : t * S + CTX], glf[t * S : t * S + CTX, r0 : r0 + H])
            total = part if total is None else total + part
        put(plan.first[name], H, total)

    grad_context("k", gk)
    grad_context("v", gv)
    due(point + 1)
    point += 2

    for t in range(T):
        swap(1, t, xs, xr_b).wait_send()
    for t in range(T):
        rows = slice(t * S, (t + 1) * S)
        ctx = slice(t * S, t * S + CTX)

        def body(j, t=t, rows=rows, ctx=ctx, point=point):
            cs = pl.ds(pl.multiple_of(j * 256, 256), 256)
            part = nt(glf[rows, gq : gq + H], wqkv[0, cs, :])
            extra = nt(glf[ctx, gk : gk + H], wqkv[1, cs, :]) + nt(glf[ctx, gv : gv + H], wqkv[2, cs, :])
            xs[ctx, cs] = (part[:CTX] + extra).astype(BF)
            xs[t * S + CTX : (t + 1) * S, cs] = part[CTX:].astype(BF)
            due_in(j, tiles, point)

        loop(tiles, body)
        swap(3, t, xs, xr_a).start()
        point += tiles

    def feed_out(t, point):
        rows = slice(t * S, (t + 1) * S)

        def body(j):
            cs = pl.ds(pl.multiple_of(j * 256, 256), 256)
            nrm[rows, cs] = nn(act[rows, :], wdown[:, cs]).astype(BF)
            due_in(j, tiles, point)

        loop(tiles, body)

    feed_out(0, point)
    point += tiles

    def first_back(b):
        rs = pl.ds(pl.multiple_of(b * NB, NB), NB)
        grad_norm = xs[rs, :].astype(F32) + xr_a[rs, :].astype(F32)
        unit, inverse = unit_rows(gl[rs, :].astype(F32))
        vec[0:1, :] += jnp.sum(grad_norm * unit, axis=0, keepdims=True)
        vec[1:2, :] += jnp.sum(grad_norm, axis=0, keepdims=True)
        gres[rs, :] = gres[rs, :] + norm_backward(grad_norm, unit, inverse, g1)

    again.wait()
    for t in range(T):
        swap(3, t, xs, xr_a).wait_recv()
        loop(S // NB, lambda i, t=t: first_back(t * (S // NB) + i))
        due(point)
        point += 1
    swap(2, 0, nrm, xr_b).start()
    store_gin = pltpu.make_async_copy(gres, gin_hbm, out_sem.at[1])
    store_gin.start()
    def norm_sums(d):
        return remote(vmine.at[d], vtheirs.at[d], vsend.at[d], vrecv.at[d], others[d - 1])

    if plan.fused:
        sums = vec[...]
        for o in range(plan.dp):
            vmine[lax.rem(o - dp + plan.dp, plan.dp)] = pltpu.roll(sums, (D - o * plan.share) % D, 1)[:, 0:128]
        for d in range(1, plan.dp):
            norm_sums(d).start()
    else:
        put(plan.first["vec"], 128, jnp.concatenate([vec[...], jnp.zeros((128 - vec.shape[0], D), F32)], axis=0).T)
    due(point)
    point += 1

    for t in range(1, T):
        feed_out(t, point)
        point += tiles
        swap(2, t, nrm, xr_b).start()

    def output(b):
        rs = rows_of(b)
        pos = lax.broadcasted_iota(jnp.int32, (RB, 1), 0) + lax.rem(b * RB, S)
        live = pos < CTX + counts_ref[lax.div(b * RB, S)]
        total = resid[rs, :] + (nrm[rs, :].astype(F32) + xr_b[rs, :].astype(F32))
        n2[rs, :] = jnp.where(live, total, 0.0).astype(BF)

    for t in range(T):
        swap(2, t, nrm, xr_b).wait_recv()
        loop(per, lambda i, t=t: output(t * per + i))
        due(point)
        point += 1
    store_out = pltpu.make_async_copy(n2, out_hbm, out_sem.at[0])
    store_out.start()
    assert point == len(SERVE)
    due(point, True)
    if plan.fused:
        total = vmine[0]
        for d in range(1, plan.dp):
            norm_sums(d).wait_recv()
            total = total + vtheirs[d]
        vmine[0] = total
        store_sums = pltpu.make_async_copy(vmine.at[0], grads_hbm[4], out_sem.at[2])
        store_sums.start()
        for d in range(1, plan.dp):
            norm_sums(d).wait_send()
        store_sums.wait()

    if not plan.fused:
        store = lambda i: pltpu.make_async_copy(g, grads_hbm[0], red_sem.at[0])
        store(0).start()
    for p in prog:
        p[1]()
    for t in range(T):
        swap(2, t, nrm, xr_b).wait_send()
        swap(3, t, xs, xr_a).wait_send()
    store_out.wait()
    store_gin.wait()
    for i in range(max(1, len(prog))):
        store(i).wait()


def run_layer(plan, counts, x, wqkv, wout, wup, wdown, cot, gains):
    R, D, H, FF, W = plan.rows, plan.width, plan.heads, plan.hidden, plan.columns
    V = pltpu.VMEM
    DMA = pltpu.SemaphoreType.DMA
    n = len(plan.chunks)
    share = plan.share
    if plan.fused:
        gshape = (2, 2, 2, 2, share, W)
        comm = [V((2, 2, 2, share, W), BF), V((2, 2, share, W), BF), V((3, share, W), BF)]
        comm += [V((2, 2, share, plan.z_columns), BF), V((share, W), F32), V((plan.dp, 8, 128), F32), V((plan.dp, 8, 128), F32)]
    else:
        gshape = (D, W)
        comm = [V((8, 128), F32)] * 7
    scratch = [
        V((R, D), BF), V((3, D, H), BF), V((H, D), BF), V((D, FF), BF), V((FF, D), BF), V((R, D), BF),
        V((R, D), BF), V((R, H), BF), V((plan.tables * CTX, H), BF), V((plan.tables * CTX, H), BF),
        V((plan.tables * (H // PAIR), 2 * CTX, plan.seq), F32), V((R, H), BF), V((R, D), F32), V((R, D), F32),
        V((D, R), BF), V((D, R), BF), V((R, FF), BF), V((R, FF), BF), V((8, D), F32), V((3, R, 256), F32), V((2 * CTX, plan.seq), BF),
        V((R, D), BF), V((R, D), BF), V((R, D), BF),
        V(gshape, BF), *comm,
        DMA((7,)), DMA((3,)), DMA((n,)), DMA((4, plan.tables)), DMA((4, plan.tables)),
        DMA((n, 5)), DMA((n, 5)), DMA((plan.dp,)), DMA((plan.dp,)),
    ]
    hbm = pl.BlockSpec(memory_space=pl.ANY)

    def kernel(*refs):
        layer_kernel(plan, *refs)

    return pl.pallas_call(
        kernel,
        out_shape=(
            jax.ShapeDtypeStruct((R, D), BF),
            jax.ShapeDtypeStruct((R, D), F32),
            *(jax.ShapeDtypeStruct(*a) for a in plan.grad_shapes),
        ),
        in_specs=[pl.BlockSpec(memory_space=pltpu.SMEM)] + [hbm] * 6 + [pl.BlockSpec(memory_space=pltpu.VMEM)] * 4,
        out_specs=(hbm,) * (2 + len(plan.grad_shapes)),
        scratch_shapes=scratch,
        compiler_params=pltpu.CompilerParams(collective_id=0, has_side_effects=True, vmem_limit_bytes=67043328),
        name="layer",
    )(counts, x, wqkv, wout, wup, wdown, cot, *gains)


def finish_kernel(plan, *refs):
    n = 6
    src, vec_ref, dst, vec_out = refs[:n], refs[n], refs[n + 1 : 2 * n + 1], refs[2 * n + 1 : 2 * n + 5]
    bufs, vec_buf, in_sem, out_sem, vec_sem = refs[2 * n + 5 : 3 * n + 5], *refs[3 * n + 5 :]
    load_vec = pltpu.make_async_copy(vec_ref, vec_buf, vec_sem)
    load_vec.start()
    moves = []
    for i in range(n):
        rows = src[i].shape[0]
        parts = plan.finish_parts[i]
        for j in range(parts):
            moves.append((i, pl.ds(j * (rows // parts), rows // parts)))
    loads, stores = [], []
    for m, (i, rows) in enumerate(moves):
        loads.append(pltpu.make_async_copy(src[i].at[rows], bufs[i].at[rows], in_sem.at[m]))
        stores.append(pltpu.make_async_copy(bufs[i].at[rows], dst[i].at[rows], out_sem.at[m]))
    for c in loads:
        c.start()
    load_vec.wait()
    for i in range(4):
        vec_out[i][...] = vec_buf[i, 0 : plan.share]
    for a, b in zip(loads, stores):
        a.wait()
        b.start()
    for c in stores:
        c.wait()


def finish(plan, shape, out, gin, down, up, o, qkv, vec):
    arrays = (gin, out, up, down, qkv, o)
    n = sum(plan.finish_parts)
    hbm = pl.BlockSpec(memory_space=pltpu.HBM)
    vmem = pl.BlockSpec(memory_space=pltpu.VMEM)
    share = plan.share

    def kernel(*refs):
        finish_kernel(plan, *refs)

    gin, out, up, down, qkv, o, *norms = pl.pallas_call(
        kernel,
        out_shape=tuple(jax.ShapeDtypeStruct(a.shape, a.dtype) for a in arrays)
        + tuple(jax.ShapeDtypeStruct((share,), F32) for _ in range(4)),
        in_specs=[hbm] * 7,
        out_specs=(hbm,) * 6 + (vmem,) * 4,
        scratch_shapes=[pltpu.VMEM(a.shape, a.dtype) for a in arrays]
        + [pltpu.VMEM(vec.shape, F32), pltpu.SemaphoreType.DMA((n,)), pltpu.SemaphoreType.DMA((n,)), pltpu.SemaphoreType.DMA],
        name="finish",
    )(*arrays, vec)
    return (out.reshape(shape), gin.reshape(shape), jnp.transpose(qkv, (1, 0, 2)), o.T, up, down.T, *norms)


def per_device(dp, inputs, counts, w_qkv, w_out, w_up, w_down, gain_one, shift_one, gain_two, shift_two, cotangent):
    tables, seq, width = inputs.shape
    heads, hidden = w_out.shape[0], w_up.shape[1]
    plan = Plan(tables, seq, width, heads, hidden, dp)
    rows = tables * seq
    gains = (gain_one, shift_one, gain_two, shift_two)
    out, gin, *grads = run_layer(
        plan,
        counts,
        inputs.reshape(rows, width),
        jnp.transpose(w_qkv, (1, 0, 2)),
        w_out,
        w_up,
        w_down,
        cotangent.reshape(rows, width),
        gains,
    )
    if plan.fused:
        down, up, o, qkv, vec = grads
        return finish(plan, inputs.shape, out, gin, down, up, o, qkv, vec)
    else:
        red = lax.psum_scatter(grads[0].astype(F32), "dp", scatter_dimension=0, tiled=True)
        at = 2 * hidden
        down, up, o = red[:, :hidden], red[:, hidden:at], red[:, at : at + heads]
        qkv = red[:, at + heads : at + 4 * heads].reshape(-1, 3, heads).transpose(1, 0, 2)
        vec = red[:, at + 4 * heads : at + 4 * heads + 4].T
    return (
        out.reshape(inputs.shape),
        gin.reshape(inputs.shape),
        jnp.transpose(qkv, (1, 0, 2)),
        o.T,
        up,
        down.T,
        vec[0],
        vec[1],
        vec[2],
        vec[3],
    )


def solution(mesh):
    dp = mesh.shape["dp"]
    in_specs = (
        P("dp", None, None), P("dp"), P(None, None, "mp"), P("mp", None), P(None, "mp"), P("mp", None),
        P(), P(), P(), P(), P("dp", None, None),
    )
    out_specs = (
        P("dp", None, None), P("dp", None, None), P("dp", None, "mp"), P("mp", "dp"), P("dp", "mp"), P("mp", "dp"),
        P("dp"), P("dp"), P("dp"), P("dp"),
    )

    def step(*args):
        return per_device(dp, *args)

    return jax.shard_map(step, mesh=mesh, in_specs=in_specs, out_specs=out_specs, check_vma=False)
```

```python
import math

import jax
import jax.numpy as jnp
from jax import lax
from jax.experimental import pallas as pl
from jax.experimental.pallas import tpu as pltpu
from jax.sharding import PartitionSpec as P

HD = 64
CTX = 384
EPS = 1e-05
BF = jnp.bfloat16
F32 = jnp.float32
MESH = pl.DeviceIdType.MESH
PAIR = 2 * HD
RB = 256
NB = 128


def nn(a, b):
    return lax.dot_general(a, b, (((1,), (0,)), ((), ())), preferred_element_type=F32)


def nt(a, b):
    return lax.dot_general(a, b, (((1,), (1,)), ((), ())), preferred_element_type=F32)


def tn(a, b):
    return lax.dot_general(a, b, (((0,), (0,)), ((), ())), preferred_element_type=F32)


def unit_rows(rows):
    centre = jnp.mean(rows, axis=-1, keepdims=True)
    centred = rows - centre
    inverse = lax.rsqrt(jnp.mean(centred * centred, axis=-1, keepdims=True) + EPS)
    return centred * inverse, inverse


def norm_backward(grad, unit, inverse, gain):
    u = grad * gain
    first = jnp.mean(u, axis=-1, keepdims=True)
    second = jnp.mean(u * unit, axis=-1, keepdims=True)
    return inverse * (u - first - unit * second)


CHUNKS = (('down', 0, 256), ('up', 0, 256), ('down', 256, 256), ('up', 256, 256), ('down', 512, 512), ('up', 512, 512), ('down', 1024, 512), ('up', 1024, 512), ('out', 0, 384), ('q', 0, 128), ('q', 128, 256), ('k', 0, 256), ('k', 256, 128), ('v', 0, 128), ('v', 128, 128), ('v', 256, 128))
HOPS = ('y', 'x', 'y', 'zy', 'x', 'zx', 'x', 'y', 'y', 'zx', 'x', 'x', 'y', 'y', 'y', 'y')
ORDER = ((0, 0), (1, 0), (3, 0), (2, 0), (0, 1), (1, 1), (5, 0), (4, 0), (3, 1), (0, 2), (1, 2), (2, 1), (7, 0), (5, 1), (6, 0), (3, 2), (4, 1), (2, 2), (7, 1), (8, 0), (3, 3), (4, 2), (5, 2), (0, 3), (1, 3), (6, 1), (2, 3), (7, 2), (10, 0), (3, 4), (8, 1), (12, 0), (9, 0), (5, 3), (13, 0), (4, 3), (6, 2), (11, 0), (14, 0), (10, 1), (12, 1), (5, 4), (7, 3), (9, 1), (8, 2), (13, 1), (15, 0), (6, 3), (14, 1), (11, 1), (9, 2), (10, 2), (12, 2), (13, 2), (14, 2), (15, 1), (9, 3), (8, 3), (11, 2), (10, 3), (15, 2), (9, 4), (12, 3), (13, 3), (14, 3), (11, 3), (15, 3))
SERVE = (2, 4, 4, 8, 9, 13, 13, 15, 17, 18, 20, 21, 23, 26, 29, 34, 35, 39, 41, 44, 47, 47, 49, 52, 53, 56, 59, 59, 61, 62, 65, 65, 65)


class Plan:
    def __init__(self, tables, seq, width, heads, hidden, dp):
        self.tables, self.seq, self.width, self.heads, self.hidden, self.dp = tables, seq, width, heads, hidden, dp
        self.rows = tables * seq
        self.share = width // dp
        self.fused = dp == 16 and self.share % 16 == 0
        self.step = 256
        self.first = {"down": 0, "up": hidden, "out": 2 * hidden}
        for name, before in (("q", "out"), ("k", "q"), ("v", "k"), ("vec", "v")):
            self.first[name] = self.first[before] + heads
        at = self.first["vec"]
        self.z_columns = 0
        self.z_at = []
        if hidden == 1536 and heads == 384:
            widths = CHUNKS
        else:
            widths = (("down", 0, hidden), ("up", 0, hidden), *((n, 0, heads) for n in ("out", "q", "k", "v")))
        chunks = [(name, self.first[name] + off, cw) for name, off, cw in widths]
        chunks = [c + (HOPS[i % len(HOPS)],) for i, c in enumerate(chunks)]
        for _, _, cw, kind in chunks:
            self.z_at.append(self.z_columns)
            self.z_columns += cw if kind[0] == "z" else 0
        self.chunks = chunks
        self.columns = at if self.fused else at + 128
        self.finish_parts = (2, 1, 1, 1, 1, 1)
        if self.fused:
            shapes = ((self.share, hidden), (self.share, hidden), (self.share, heads), (3, self.share, heads), (8, 128))
            self.grad_shapes = tuple((a, F32) for a in shapes)
        else:
            self.grad_shapes = (((width, self.columns), BF),)


def layer_kernel(
    plan,
    counts_ref, x_hbm, wqkv_hbm, wout_hbm, wup_hbm, wdown_hbm, cot_hbm, g1_ref, b1_ref, g2_ref, b2_ref,
    out_hbm, gin_hbm, *rest,
):
    grads_hbm, rest = rest[: len(plan.grad_shapes)], rest[len(plan.grad_shapes) :]
    (
        x, wqkv, wout, wup, wdown, gl,
    nrm, q, k, v, prob, ho, resid, gres, glt, n2t, act, glf, vec, work, low_s,
    xs, xr_a, xr_b,
    g, r1, r2, r3, r4, red, vmine, vtheirs,
    in_sem, out_sem, red_sem, xsend, xrecv, send, recv, vsend, vrecv,
    ) = rest
    T, S, D, H, FF = plan.tables, plan.seq, plan.width, plan.heads, plan.hidden
    R = plan.rows
    pairs = H // PAIR
    dp = lax.axis_index("dp")
    mp = lax.axis_index("mp")
    xx, yy, zz = lax.rem(dp, 2), lax.rem(lax.div(dp, 2), 2), lax.div(dp, 4)
    partner = (dp, 1 - mp)

    def chip(z, y, x_):
        return (z * 4 + y * 2 + x_, mp)

    x_peer, y_peer = chip(zz, yy, 1 - xx), chip(zz, 1 - yy, xx)
    z_peers = [chip(lax.rem(zz + d, 4), yy, xx) for d in (1, 2, 3)]
    others = [(lax.rem(dp + d, plan.dp), mp) for d in range(1, plan.dp)] if plan.fused else []
    peers = [partner] + others

    loads = [
        pltpu.make_async_copy(a, b, in_sem.at[i])
        for i, (a, b) in enumerate(
            ((x_hbm, x), (wqkv_hbm, wqkv), (wout_hbm, wout), (cot_hbm, gl), (wup_hbm, wup), (wdown_hbm, wdown))
        )
    ]
    for c in loads[:2]:
        c.start()
    barrier = pltpu.get_barrier_semaphore()
    for n in peers:
        pl.semaphore_signal(barrier, inc=1, device_id=n, device_id_type=MESH)

    def remote(src, dst, ss, rs, dev):
        return pltpu.make_async_remote_copy(src, dst, ss, rs, device_id=dev, device_id_type=MESH)

    def swap(i, t, src, dst):
        rows = pl.ds(t * S, S)
        return remote(src.at[rows], dst.at[rows], xsend.at[i, t], xrecv.at[i, t], partner)

    zh, zl = lax.div(zz, 2), lax.rem(zz, 2)
    outer = lax.rem(zh + zl + 1, 2)

    def store(i):
        name, c0, cw, _ = plan.chunks[i]
        off = c0 - plan.first[name]
        at = {"down": 0, "up": 1, "out": 2, "q": 3, "k": 3, "v": 3}[name]
        dst = grads_hbm[at].at["qkv".index(name)] if at == 3 else grads_hbm[at]
        return pltpu.make_async_copy(red.at[:, pl.ds(c0, cw)], dst.at[:, pl.ds(off, cw)], red_sem.at[i])

    def finished(i, total):
        _, c0, cw, _ = plan.chunks[i]
        red[:, pl.ds(c0, cw)] = total
        store(i).start()

    def add(dst, a, b):
        dst[...] = (a[...].astype(F32) + b[...].astype(F32)).astype(BF)

    def flat(i):
        _, c0, cw, kind = plan.chunks[i]
        cs = pl.ds(c0, cw)
        isx = kind == "x"
        other, mine = (1 - yy, yy) if isx else (1 - xx, xx)
        c1 = remote(
            g.at[:, :, :, 1 - xx, :, cs] if isx else g.at[:, :, 1 - yy, :, :, cs],
            r1.at[:, :, :, :, cs], send.at[i, 0], recv.at[i, 0], x_peer if isx else y_peer,
        )
        c2 = remote(r1.at[:, :, other, :, cs], r2.at[:, :, :, cs], send.at[i, 1], recv.at[i, 1], y_peer if isx else x_peer)
        c3 = []
        for d in (1, 2, 3):
            z = lax.rem(zz + d, 4)
            c3.append(
                remote(r2.at[lax.div(z, 2), lax.rem(z, 2), :, cs], r3.at[d - 1, :, cs], send.at[i, 1 + d], recv.at[i, 1 + d], z_peers[d - 1])
            )

        def add_one():
            c1.wait_recv()

            def part(p):
                def one(j):
                    h, l = lax.div(j, 2), lax.rem(j, 2)
                    own = g.at[h, l, p, xx, :, cs] if isx else g.at[h, l, yy, p, :, cs]
                    add(r1.at[h, l, p, :, cs], own, r1.at[h, l, p, :, cs])

                loop(4, one)

            part(other)
            c2.start()
            part(mine)

        def add_two():
            c2.wait_recv()
            for d in (2, 3, 1, 0):
                z = lax.rem(zz + d, 4)
                h, l = lax.div(z, 2), lax.rem(z, 2)
                add(r2.at[h, l, :, cs], r1.at[h, l, mine, :, cs], r2.at[h, l, :, cs])
                if d:
                    c3[d - 1].start()

        def add_three():
            for c in c3:
                c.wait_recv()
            total = r2[zh, zl, :, cs].astype(F32)
            for d in range(3):
                total = total + r3[d, :, cs].astype(F32)
            finished(i, total)

        def drain():
            for c in (c1, c2, *c3):
                c.wait_send()

        return [c1.start, add_one, add_two, add_three], drain

    def upright(i):
        _, c0, cw, kind = plan.chunks[i]
        cs, zs = pl.ds(c0, cw), pl.ds(plan.z_at[i], cw)
        isx = kind == "zx"
        kept = jnp.where(outer == 1, zh, 1 - zh)
        mate = chip(zh * 2 + 1 - zl, yy, xx)
        across_mid = chip(3 - zz, yy, xx)
        across_end = chip((1 - zh) * 3, yy, xx)
        ca = remote(g.at[1 - kept, :, :, :, :, cs], r1.at[:, :, :, :, cs], send.at[i, 0], recv.at[i, 0], mate)
        end_b = remote(r1.at[1 - zl, :, :, :, cs], r4.at[:, :, :, zs], send.at[i, 1], recv.at[i, 1], mate)
        mid_b = remote(r1.at[1 - zl, :, :, :, cs], r2.at[:, :, :, cs], send.at[i, 1], recv.at[i, 2], across_mid)
        far_b = remote(r1.at[zl, :, :, :, cs], r2.at[:, :, :, cs], send.at[i, 2], recv.at[i, 2], across_end)
        if isx:
            half, single = r2.at[:, 1 - xx, :, cs], r2.at[1 - yy, xx, :, cs]
        else:
            half, single = r2.at[1 - yy, :, :, cs], r2.at[yy, 1 - xx, :, cs]
        cc = remote(half, r3.at[0:2, :, cs], send.at[i, 3], recv.at[i, 3], x_peer if isx else y_peer)
        cd = remote(single, r3.at[2, :, cs], send.at[i, 4], recv.at[i, 4], y_peer if isx else x_peer)

        def add_one():
            ca.wait_recv()

            def one(j):
                l, y, x_ = lax.div(j, 4), lax.rem(lax.div(j, 2), 2), lax.rem(j, 2)
                add(r1.at[l, y, x_, :, cs], g.at[kept, l, y, x_, :, cs], r1.at[l, y, x_, :, cs])

            loop(8, one)

            @pl.when(outer == 1)
            def _():
                end_b.start()

            @pl.when(outer == 0)
            def _():
                mid_b.start()
                far_b.start()

        def add_two():
            mid_b.wait_recv()

            @pl.when(outer == 0)
            def _():
                end_b.wait_recv()

            def part(y, x_):
                @pl.when(outer == 1)
                def _():
                    add(r2.at[y, x_, :, cs], r1.at[zl, y, x_, :, cs], r2.at[y, x_, :, cs])

                @pl.when(outer == 0)
                def _():
                    add(r2.at[y, x_, :, cs], r4.at[y, x_, :, zs], r2.at[y, x_, :, cs])

            for p in range(2):
                part(p, 1 - xx) if isx else part(1 - yy, p)
            cc.start()
            for p in range(2):
                part(p, xx) if isx else part(yy, p)

        def add_three():
            cc.wait_recv()

            def part(p):
                at = r2.at[p, xx, :, cs] if isx else r2.at[yy, p, :, cs]
                add(at, at, r3.at[p, :, cs])

            other, mine = (1 - yy, yy) if isx else (1 - xx, xx)
            part(other)
            cd.start()
            part(mine)

        def add_four():
            cd.wait_recv()
            finished(i, r2[yy, xx, :, cs].astype(F32) + r3[2, :, cs].astype(F32))

        def drain():
            ca.wait_send()

            @pl.when(outer == 1)
            def _():
                end_b.wait_send()

            @pl.when(outer == 0)
            def _():
                mid_b.wait_send()
                far_b.wait_send()

            cc.wait_send()
            cd.wait_send()

        return [ca.start, add_one, add_two, add_three, add_four], drain

    prog = []
    if plan.fused:
        prog = [upright(i) if c[3][0] == "z" else flat(i) for i, c in enumerate(plan.chunks)]

    def due(first, last=None):
        if plan.fused:
            start = SERVE[first - 1] if first else 0
            for i, stage in ORDER[start : SERVE[first] if last is None else len(ORDER)]:
                prog[i][0][stage]()

    def due_in(j, n, first, stride=1):
        for i in range(n):
            if plan.fused and SERVE[first + i * stride] > (SERVE[first + i * stride - 1] if first + i * stride else 0):
                pl.when(j == i)(lambda i=i: due(first + i * stride))

    def loop(n, body):
        def step(i, carry):
            body(i)
            return carry

        lax.fori_loop(0, n, step, 0)

    def put(c0, cw, rows768):
        cs = pl.ds(c0, cw)
        if plan.fused:
            g[:, :, :, :, :, cs] = rows768.astype(BF).reshape(2, 2, 2, 2, plan.share, cw)
        else:
            g[:, cs] = rows768.astype(BF)

    def rows_of(b):
        return pl.ds(pl.multiple_of(b * RB, RB), RB)

    loads[0].wait()
    for c in loads[2:]:
        c.start()
    g1, b1, g2, b2 = (a[...].reshape(1, D) for a in (g1_ref, b1_ref, g2_ref, b2_ref))

    def first_norm(b):
        rs = rows_of(b)
        unit, _ = unit_rows(x[rs, :].astype(F32))
        nrm[rs, :] = (unit * g1 + b1).astype(BF)

    per = S // RB
    for t in range(T):
        for i in range(per):
            first_norm(t * per + i)
        if t == 0:
            loads[1].wait()
        rows, context, kept = slice(t * S, (t + 1) * S), slice(t * S, t * S + CTX), slice(t * CTX, (t + 1) * CTX)
        q[rows, :] = nn(nrm[rows, :], wqkv[0]).astype(BF)
        k[kept, :] = nn(nrm[context, :], wqkv[1]).astype(BF)
        v[kept, :] = nn(nrm[context, :], wqkv[2]).astype(BF)

    n2 = x
    low_p = n2.at[0 : 2 * CTX, 0:S]

    scale = 1.0 / math.sqrt(HD)
    low_lane = lax.broadcasted_iota(jnp.int32, (CTX, PAIR), 1) < HD
    low_row = lax.broadcasted_iota(jnp.int32, (PAIR, CTX), 0) < HD

    def stacked(a):
        zero = jnp.zeros_like(a)
        return jnp.concatenate([jnp.where(low_lane, a, zero), jnp.where(low_lane, zero, a)], axis=0)

    def beside(a):
        at = a.T
        zero = jnp.zeros_like(at)
        return jnp.concatenate([jnp.where(low_row, at, zero), jnp.where(low_row, zero, at)], axis=1)

    def merged(a):
        return jnp.where(low_lane, a[:CTX], a[CTX:])

    def attend_scores(t, h):
        rows, kept, cols = slice(t * S, (t + 1) * S), slice(t * CTX, (t + 1) * CTX), slice(h * PAIR, (h + 1) * PAIR)
        prob[t * pairs + h] = nt(stacked(k[kept, cols]), q[rows, cols])

    def attend(t, h):
        rows, kept, cols = slice(t * S, (t + 1) * S), slice(t * CTX, (t + 1) * CTX), slice(h * PAIR, (h + 1) * PAIR)
        slot = t * pairs + h
        for i in range(2):
            part = slice(i * CTX, (i + 1) * CTX)
            s = prob[slot, part, :]
            e = jnp.exp2((s - jnp.max(s, axis=0, keepdims=True)) * (scale * math.log2(math.e)))
            p = e * (1.0 / jnp.sum(e, axis=0, keepdims=True))
            prob[slot, part, :] = p
            low_s[part, :] = p.astype(BF)
        ho[rows, cols] = nn(beside(v[kept, cols]), low_s[...]).T.astype(BF)

    order = [(t, h) for t in range(T) for h in range(pairs)]
    attend_scores(*order[0])
    for j, (t, h) in enumerate(order):
        if j + 1 < len(order):
            attend_scores(*order[j + 1])
        attend(t, h)
        if h == pairs - 1:
            if t == 0:
                loads[2].wait()
                pl.semaphore_wait(barrier, len(peers))
            rows = slice(t * S, (t + 1) * S)
            xs[rows, :] = nn(ho[rows, :], wout[...]).astype(BF)
            swap(0, t, xs, xr_a).start()

    loads[3].wait()

    def mask(b):
        rs = rows_of(b)
        pos = lax.broadcasted_iota(jnp.int32, (RB, 1), 0) + lax.rem(b * RB, S)
        live = pos < CTX + counts_ref[lax.div(b * RB, S)]
        kept = jnp.where(live, gl[rs, :].astype(F32), 0.0).astype(BF)
        gl[rs, :] = kept
        glt[:, rs] = kept.T

    loop(R // RB, mask)

    def second_norm(b):
        rs = rows_of(b)
        r = x[rs, :].astype(F32) + (xs[rs, :].astype(F32) + xr_a[rs, :].astype(F32))
        resid[rs, :] = r
        unit, _ = unit_rows(r)
        n2[rs, :] = (unit * g2 + b2).astype(BF)

    for t in range(T):
        swap(0, t, xs, xr_a).wait_recv()
        for i in range(per):
            second_norm(t * per + i)
        for b in range(t * per, (t + 1) * per):
            n2t[:, b * RB : (b + 1) * RB] = n2[b * RB : (b + 1) * RB, :].T
    loads[4].wait()
    loads[5].wait()

    step = plan.step
    steps = FF // step

    def hidden_of(c):
        return pl.ds(c * step if isinstance(c, int) else pl.multiple_of(c * step, step), step)

    def lift(c):
        work[0] = nn(n2[...], wup[:, hidden_of(c)])

    def pull(c):
        work[1] = nt(gl[...], wdown[hidden_of(c), :])

    def bend(c):
        cs = hidden_of(c)
        for b in range(R // RB):
            rs = slice(b * RB, (b + 1) * RB)
            lifted = work[0, rs, :]
            half = 0.5 + 0.5 * lax.erf(lifted * (1.0 / math.sqrt(2.0)))
            act[rs, cs] = (lifted * half).astype(BF)
            work[2, rs, :] = half + lifted * (jnp.exp(-0.5 * lifted * lifted) * (1.0 / math.sqrt(2.0 * math.pi)))

    def slope(c):
        cs = hidden_of(c)
        for b in range(R // RB):
            rs = slice(b * RB, (b + 1) * RB)
            glf[rs, cs] = (work[2, rs, :] * work[1, rs, :]).astype(BF)

    def grad(c0, left_t, right, cols, cw):
        put(c0, cw, nn(left_t[...], right[:, cols]))

    def feed(c):
        off = pl.multiple_of(c * step, step)
        lift(c)
        pull(c)
        bend(c)
        grad(plan.first["down"] + off, glt, act, hidden_of(c), step)
        slope(c)
        grad(plan.first["up"] + off, n2t, glf, hidden_of(c), step)
        due_in(c, steps, 0)

    loop(steps, feed)
    point = steps

    for t in range(T):
        swap(0, t, xs, xr_a).wait_send()
    tiles = D // 256
    for t in range(T):
        rows = slice(t * S, (t + 1) * S)

        def body(j, rows=rows):
            cs = pl.ds(pl.multiple_of(j * 256, 256), 256)
            xs[rows, cs] = nt(glf[rows, :], wup[cs, :]).astype(BF)

        loop(tiles, body)
        swap(1, t, xs, xr_b).start()
        due(point)
        point += 1

    vec[...] = jnp.zeros_like(vec)

    def second_back(b):
        rs = pl.ds(pl.multiple_of(b * NB, NB), NB)
        grad_norm = xs[rs, :].astype(F32) + xr_b[rs, :].astype(F32)
        unit, inverse = unit_rows(resid[rs, :])
        vec[2:3, :] += jnp.sum(grad_norm * unit, axis=0, keepdims=True)
        vec[3:4, :] += jnp.sum(grad_norm, axis=0, keepdims=True)
        total = gl[rs, :].astype(F32) + norm_backward(grad_norm, unit, inverse, g2)
        gres[rs, :] = total
        gl[rs, :] = total.astype(BF)

    for t in range(T):
        swap(1, t, xs, xr_b).wait_recv()
        loop(S // NB, lambda i, t=t: second_back(t * (S // NB) + i))
        due(point)
        point += 1

    gh, gq, gk, gv = 0, H, 2 * H, 3 * H
    for t in range(T):
        rows = slice(t * S, (t + 1) * S)
        glf[rows, gh : gh + H] = nt(gl[rows, :], wout[...]).astype(BF)
    put(plan.first["out"], H, tn(gl[...], ho[...]))
    again = pltpu.make_async_copy(x_hbm, gl, in_sem.at[6])
    again.start()
    due(point)
    point += 1

    half = S // 2

    def back_scores(j, i):
        t, h = order[j]
        rows, kept, cols = slice(t * S, (t + 1) * S), slice(t * CTX, (t + 1) * CTX), slice(h * PAIR, (h + 1) * PAIR)
        part = slice(t * S + i * half, t * S + (i + 1) * half)
        work[(2 * j + i) % 3, 0 : 2 * CTX, :] = nt(stacked(v[kept, cols]), glf[part, gh + h * PAIR : gh + (h + 1) * PAIR])

    def attend_back(j):
        t, h = order[j]
        rows, context = slice(t * S, (t + 1) * S), slice(t * S, t * S + CTX)
        kept, cols = slice(t * CTX, (t + 1) * CTX), slice(h * PAIR, (h + 1) * PAIR)
        for i in range(2):
            if j + 1 < len(order):
                back_scores(j + 1, i)
            side = slice(i * half, (i + 1) * half)
            for n in range(2):
                part = slice(n * CTX, (n + 1) * CTX)
                p = prob[j, part, side]
                b = work[(2 * j + i) % 3, part, :]
                low_p[part, side] = p.astype(BF)
                low_s[part, side] = (p * (b - jnp.sum(p * b, axis=0, keepdims=True))).astype(BF)

        def at(first):
            return slice(first + h * PAIR, first + (h + 1) * PAIR)

        glf[rows, at(gq)] = (nn(beside(k[kept, cols]), low_s[...]).T * scale).astype(BF)
        glf[context, at(gk)] = (merged(nn(low_s[...], q[rows, cols])) * scale).astype(BF)
        glf[context, at(gv)] = merged(nn(low_p[...], glf[rows, at(gh)])).astype(BF)

    back_scores(0, 0)
    back_scores(0, 1)
    for j in range(len(order)):
        attend_back(j)
        if j % 2 == 1:
            due(point)
            point += 1

    for b in range(R // RB):
        n2t[:, b * RB : (b + 1) * RB] = nrm[b * RB : (b + 1) * RB, :].T
    grad(plan.first["q"], n2t, glf, slice(gq, gq + H), H)
    due(point)

    def grad_context(name, r0):
        total = None
        for t in range(T):
            part = nn(n2t[:, t * S : t * S + CTX], glf[t * S : t * S + CTX, r0 : r0 + H])
            total = part if total is None else total + part
        put(plan.first[name], H, total)

    grad_context("k", gk)
    grad_context("v", gv)
    due(point + 1)
    point += 2

    for t in range(T):
        swap(1, t, xs, xr_b).wait_send()
    for t in range(T):
        rows = slice(t * S, (t + 1) * S)
        ctx = slice(t * S, t * S + CTX)

        def body(j, t=t, rows=rows, ctx=ctx, point=point):
            cs = pl.ds(pl.multiple_of(j * 256, 256), 256)
            part = nt(glf[rows, gq : gq + H], wqkv[0, cs, :])
            extra = nt(glf[ctx, gk : gk + H], wqkv[1, cs, :]) + nt(glf[ctx, gv : gv + H], wqkv[2, cs, :])
            xs[ctx, cs] = (part[:CTX] + extra).astype(BF)
            xs[t * S + CTX : (t + 1) * S, cs] = part[CTX:].astype(BF)
            due_in(j, tiles, point)

        loop(tiles, body)
        swap(3, t, xs, xr_a).start()
        point += tiles

    def feed_out(t, point):
        rows = slice(t * S, (t + 1) * S)

        def body(j):
            cs = pl.ds(pl.multiple_of(j * 256, 256), 256)
            nrm[rows, cs] = nn(act[rows, :], wdown[:, cs]).astype(BF)
            due_in(j, tiles, point)

        loop(tiles, body)

    feed_out(0, point)
    point += tiles

    def first_back(b):
        rs = pl.ds(pl.multiple_of(b * NB, NB), NB)
        grad_norm = xs[rs, :].astype(F32) + xr_a[rs, :].astype(F32)
        unit, inverse = unit_rows(gl[rs, :].astype(F32))
        vec[0:1, :] += jnp.sum(grad_norm * unit, axis=0, keepdims=True)
        vec[1:2, :] += jnp.sum(grad_norm, axis=0, keepdims=True)
        gres[rs, :] = gres[rs, :] + norm_backward(grad_norm, unit, inverse, g1)

    again.wait()
    for t in range(T):
        swap(3, t, xs, xr_a).wait_recv()
        loop(S // NB, lambda i, t=t: first_back(t * (S // NB) + i))
        due(point)
        point += 1
    swap(2, 0, nrm, xr_b).start()
    store_gin = pltpu.make_async_copy(gres, gin_hbm, out_sem.at[1])
    store_gin.start()
    def norm_sums(d):
        return remote(vmine.at[d], vtheirs.at[d], vsend.at[d], vrecv.at[d], others[d - 1])

    if plan.fused:
        sums = vec[...]
        for o in range(plan.dp):
            vmine[lax.rem(o - dp + plan.dp, plan.dp)] = pltpu.roll(sums, (D - o * plan.share) % D, 1)[:, 0:128]
        for d in range(1, plan.dp):
            norm_sums(d).start()
    else:
        put(plan.first["vec"], 128, jnp.concatenate([vec[...], jnp.zeros((128 - vec.shape[0], D), F32)], axis=0).T)
    due(point)
    point += 1

    for t in range(1, T):
        feed_out(t, point)
        point += tiles
        swap(2, t, nrm, xr_b).start()

    def output(b):
        rs = rows_of(b)
        pos = lax.broadcasted_iota(jnp.int32, (RB, 1), 0) + lax.rem(b * RB, S)
        live = pos < CTX + counts_ref[lax.div(b * RB, S)]
        total = resid[rs, :] + (nrm[rs, :].astype(F32) + xr_b[rs, :].astype(F32))
        n2[rs, :] = jnp.where(live, total, 0.0).astype(BF)

    for t in range(T):
        swap(2, t, nrm, xr_b).wait_recv()
        loop(per, lambda i, t=t: output(t * per + i))
        due(point)
        point += 1
    store_out = pltpu.make_async_copy(n2, out_hbm, out_sem.at[0])
    store_out.start()
    assert point == len(SERVE)
    due(point, True)
    if plan.fused:
        total = vmine[0]
        for d in range(1, plan.dp):
            norm_sums(d).wait_recv()
            total = total + vtheirs[d]
        vmine[0] = total
        store_sums = pltpu.make_async_copy(vmine.at[0], grads_hbm[4], out_sem.at[2])
        store_sums.start()
        for d in range(1, plan.dp):
            norm_sums(d).wait_send()
        store_sums.wait()

    if not plan.fused:
        store = lambda i: pltpu.make_async_copy(g, grads_hbm[0], red_sem.at[0])
        store(0).start()
    for p in prog:
        p[1]()
    for t in range(T):
        swap(2, t, nrm, xr_b).wait_send()
        swap(3, t, xs, xr_a).wait_send()
    store_out.wait()
    store_gin.wait()
    for i in range(max(1, len(prog))):
        store(i).wait()


def run_layer(plan, counts, x, wqkv, wout, wup, wdown, cot, gains):
    R, D, H, FF, W = plan.rows, plan.width, plan.heads, plan.hidden, plan.columns
    V = pltpu.VMEM
    DMA = pltpu.SemaphoreType.DMA
    n = len(plan.chunks)
    share = plan.share
    if plan.fused:
        gshape = (2, 2, 2, 2, share, W)
        comm = [V((2, 2, 2, share, W), BF), V((2, 2, share, W), BF), V((3, share, W), BF)]
        comm += [V((2, 2, share, plan.z_columns), BF), V((share, W), F32), V((plan.dp, 8, 128), F32), V((plan.dp, 8, 128), F32)]
    else:
        gshape = (D, W)
        comm = [V((8, 128), F32)] * 7
    scratch = [
        V((R, D), BF), V((3, D, H), BF), V((H, D), BF), V((D, FF), BF), V((FF, D), BF), V((R, D), BF),
        V((R, D), BF), V((R, H), BF), V((plan.tables * CTX, H), BF), V((plan.tables * CTX, H), BF),
        V((plan.tables * (H // PAIR), 2 * CTX, plan.seq), F32), V((R, H), BF), V((R, D), F32), V((R, D), F32),
        V((D, R), BF), V((D, R), BF), V((R, FF), BF), V((R, FF), BF), V((8, D), F32), V((3, R, 256), F32), V((2 * CTX, plan.seq), BF),
        V((R, D), BF), V((R, D), BF), V((R, D), BF),
        V(gshape, BF), *comm,
        DMA((7,)), DMA((3,)), DMA((n,)), DMA((4, plan.tables)), DMA((4, plan.tables)),
        DMA((n, 5)), DMA((n, 5)), DMA((plan.dp,)), DMA((plan.dp,)),
    ]
    hbm = pl.BlockSpec(memory_space=pl.ANY)

    def kernel(*refs):
        layer_kernel(plan, *refs)

    return pl.pallas_call(
        kernel,
        out_shape=(
            jax.ShapeDtypeStruct((R, D), BF),
            jax.ShapeDtypeStruct((R, D), F32),
            *(jax.ShapeDtypeStruct(*a) for a in plan.grad_shapes),
        ),
        in_specs=[pl.BlockSpec(memory_space=pltpu.SMEM)] + [hbm] * 6 + [pl.BlockSpec(memory_space=pltpu.VMEM)] * 4,
        out_specs=(hbm,) * (2 + len(plan.grad_shapes)),
        scratch_shapes=scratch,
        compiler_params=pltpu.CompilerParams(collective_id=0, has_side_effects=True, vmem_limit_bytes=67043328),
        name="layer",
    )(counts, x, wqkv, wout, wup, wdown, cot, *gains)


def finish_kernel(plan, *refs):
    n = 6
    src, vec_ref, dst, vec_out = refs[:n], refs[n], refs[n + 1 : 2 * n + 1], refs[2 * n + 1 : 2 * n + 5]
    bufs, vec_buf, in_sem, out_sem, vec_sem, row_sem = refs[2 * n + 5 : 3 * n + 5], *refs[3 * n + 5 : 3 * n + 10]
    rows_buf = refs[3 * n + 10 :]
    load_vec = pltpu.make_async_copy(vec_ref, vec_buf, vec_sem)
    load_vec.start()
    moves = []
    for i in range(n):
        rows = src[i].shape[0]
        parts = plan.finish_parts[i]
        for j in range(parts):
            moves.append((i, pl.ds(j * (rows // parts), rows // parts)))
    loads, stores = [], []
    for m, (i, rows) in enumerate(moves):
        loads.append(pltpu.make_async_copy(src[i].at[rows], bufs[i].at[rows], in_sem.at[m]))
        stores.append(pltpu.make_async_copy(bufs[i].at[rows], dst[i].at[rows], out_sem.at[m]))
    for c in loads:
        c.start()
    load_vec.wait()
    for i in range(4):
        rows_buf[i][...] = vec_buf[i, 0 : plan.share]
        stores.append(pltpu.make_async_copy(rows_buf[i], vec_out[i], row_sem.at[i]))
        stores[-1].start()
    for a, b in zip(loads, stores):
        a.wait()
        b.start()
    for c in stores:
        c.wait()


def finish(plan, shape, out, gin, down, up, o, qkv, vec):
    arrays = (gin, out, up, down, qkv, o)
    n = sum(plan.finish_parts)
    hbm = pl.BlockSpec(memory_space=pltpu.HBM)
    vmem = pl.BlockSpec(memory_space=pltpu.VMEM)
    share = plan.share

    def kernel(*refs):
        finish_kernel(plan, *refs)

    gin, out, up, down, qkv, o, *norms = pl.pallas_call(
        kernel,
        out_shape=tuple(jax.ShapeDtypeStruct(a.shape, a.dtype) for a in arrays)
        + tuple(jax.ShapeDtypeStruct((share,), F32) for _ in range(4)),
        in_specs=[hbm] * 7,
        out_specs=(hbm,) * 10,
        scratch_shapes=[pltpu.VMEM(a.shape, a.dtype) for a in arrays]
        + [pltpu.VMEM(vec.shape, F32), pltpu.SemaphoreType.DMA((n,)), pltpu.SemaphoreType.DMA((n,)), pltpu.SemaphoreType.DMA, pltpu.SemaphoreType.DMA((4,))]
        + [pltpu.VMEM((share,), F32)] * 4,
        name="finish",
    )(*arrays, vec)
    return (out.reshape(shape), gin.reshape(shape), jnp.transpose(qkv, (1, 0, 2)), o.T, up, down.T, *norms)


def per_device(dp, inputs, counts, w_qkv, w_out, w_up, w_down, gain_one, shift_one, gain_two, shift_two, cotangent):
    tables, seq, width = inputs.shape
    heads, hidden = w_out.shape[0], w_up.shape[1]
    plan = Plan(tables, seq, width, heads, hidden, dp)
    rows = tables * seq
    gains = (gain_one, shift_one, gain_two, shift_two)
    out, gin, *grads = run_layer(
        plan,
        counts,
        inputs.reshape(rows, width),
        jnp.transpose(w_qkv, (1, 0, 2)),
        w_out,
        w_up,
        w_down,
        cotangent.reshape(rows, width),
        gains,
    )
    if plan.fused:
        down, up, o, qkv, vec = grads
        return finish(plan, inputs.shape, out, gin, down, up, o, qkv, vec)
    else:
        red = lax.psum_scatter(grads[0].astype(F32), "dp", scatter_dimension=0, tiled=True)
        at = 2 * hidden
        down, up, o = red[:, :hidden], red[:, hidden:at], red[:, at : at + heads]
        qkv = red[:, at + heads : at + 4 * heads].reshape(-1, 3, heads).transpose(1, 0, 2)
        vec = red[:, at + 4 * heads : at + 4 * heads + 4].T
    return (
        out.reshape(inputs.shape),
        gin.reshape(inputs.shape),
        jnp.transpose(qkv, (1, 0, 2)),
        o.T,
        up,
        down.T,
        vec[0],
        vec[1],
        vec[2],
        vec[3],
    )


def solution(mesh):
    dp = mesh.shape["dp"]
    in_specs = (
        P("dp", None, None), P("dp"), P(None, None, "mp"), P("mp", None), P(None, "mp"), P("mp", None),
        P(), P(), P(), P(), P("dp", None, None),
    )
    out_specs = (
        P("dp", None, None), P("dp", None, None), P("dp", None, "mp"), P("mp", "dp"), P("dp", "mp"), P("mp", "dp"),
        P("dp"), P("dp"), P("dp"), P("dp"),
    )

    def step(*args):
        return per_device(dp, *args)

    return jax.shard_map(step, mesh=mesh, in_specs=in_specs, out_specs=out_specs, check_vma=False)
```
